256 devices in a mesh: leaf: 64 (over x, z, core), front: 4 (over y).
Axes of the slice: x: 4, y: 4, z: 8, core: 2. Of those that a mesh axis runs over, the one named last changes fastest.
Arguments:
- child_update: bfloat16 [64, 4, 1, 3, 256, 3072], P('leaf', 'front'), may hold values from -60 to 60, as said below
- sep_one: bfloat16 [64, 4, 1, 4, 256, 512], P('leaf', 'front'), may hold values from -60 to 60, as said below
- sep_two: bfloat16 [64, 4, 1, 4, 256, 256], P('leaf', 'front'), may hold values from -60 to 60, as said below
- map_one: int32 [64, 1, 4, 3], replicated, may hold values from 0 to 3, as said below
- map_two: int32 [32, 1, 4, 3], replicated, may hold values from 0 to 3, as said below
- mask_one: int32 [32, 1, 12, 4], replicated, may hold values 0 or 1
- mask_two: int32 [16, 1, 12, 4], replicated, may hold values 0 or 1
Outputs:
- factor_one: float32 [64, 4, 1, 4, 256, 512], P('leaf', 'front')
- factor_two: float32 [64, 4, 1, 4, 256, 256], P('leaf', 'front')
- update_two: bfloat16 [64, 4, 1, 3, 256, 768], P('leaf', 'front')
The draws below stay inside these ranges and needn't reach their ends.
Inputs may be any that keep to these rules, and one draw needn't show every extreme that they name: `child_update`: every child[l,b] is symmetric positive definite. `sep_one`: the top 1024 rows of each front's initial entries form a symmetric positive definite block, and every assembled front is positive definite. `sep_two`: the top 1024 rows of each front's initial entries form a symmetric positive definite block, and every assembled front is positive definite. `map_one`: for each child, batch and j the 3 entries are distinct; the two children 2p and 2p + 1 leave out different slots, so every parent tile receives one or two child tiles. `map_two`: for each first-level front, batch and j the 3 entries are distinct; fronts 2q and 2q + 1 leave out different slots, so every parent tile receives one or two child tiles.
All inputs are finite; a program needn't handle non-finite values.
Results may differ from the reference program's by a relative error of at most 0.0047.
Values may be sent and summed in bfloat16 or wider, within the bound.
A program may use at most 192 MiB of HBM per device.

```python
import math
import jax
import jax.numpy as jnp
from jax import lax

TILE = 256
ST = 4
UT = 12
BATCH = 1
S = 1024
U = 3072
F = 4096
PT = 4
CT = 3
N_LEAF = 64
N_FRONT = 4


def spread_block(key, matrix_order, diagonal_shift, gram_weight):
    key_factor = jax.random.fold_in(key, 0)
    factor_draw = jax.random.normal(key_factor, (BATCH, matrix_order, matrix_order), jnp.float32)
    scaled = factor_draw
    gram = jnp.einsum('bik,bjk->bij', scaled, scaled, precision=lax.Precision.HIGHEST) * (gram_weight / matrix_order)
    gram = 0.5 * (gram + jnp.swapaxes(gram, 1, 2))
    identity = jnp.eye(matrix_order, dtype=jnp.float32)
    return gram + diagonal_shift * identity[None, :, :]


def draw_child_update(key, part):

    def single(leaf_number):
        return spread_block(jax.random.fold_in(key, leaf_number), U, 0.5, 2.5)
    stacked = lax.map(single, jnp.arange(N_LEAF))
    shaped = stacked.reshape(N_LEAF, BATCH, CT, N_FRONT, TILE, U)
    return jnp.transpose(shaped, (0, 3, 1, 2, 4, 5)).astype(jnp.bfloat16)


def draw_entries(key, groups, strength):
    fronts = N_LEAF // groups
    deviation = strength / (math.sqrt(U) + math.sqrt(S))

    def single(front_number):
        key_top, key_low = jax.random.split(jax.random.fold_in(key, front_number))
        separator_block = spread_block(key_top, S, 2.5, 2.5)
        coupling = deviation * jax.random.normal(key_low, (BATCH, U, S), jnp.float32)
        return jnp.concatenate([separator_block, coupling], axis=1)
    stacked = lax.map(single, jnp.arange(fronts))
    shaped = stacked.reshape(fronts, BATCH, PT, N_FRONT, TILE, groups, S // groups)
    return jnp.transpose(shaped, (0, 5, 3, 1, 2, 4, 6)).reshape(N_LEAF, N_FRONT, BATCH, PT, TILE, S // groups)


def draw_sep_one(key, part):
    return draw_entries(jax.random.fold_in(key, 11), 2, 1.0).astype(jnp.bfloat16)


def draw_sep_two(key, part):
    return draw_entries(jax.random.fold_in(key, 23), 4, 0.8).astype(jnp.bfloat16)


def draw_tile_maps(key, fronts):
    key_first, key_offset, key_order = jax.random.split(key, 3)
    omitted_first = jax.random.randint(key_first, (fronts, BATCH, N_FRONT), 0, PT)
    offset_draw = jax.random.randint(key_offset, (fronts, BATCH, N_FRONT), 1, PT)
    second = (omitted_first + offset_draw) % PT
    omitted = jnp.stack([omitted_first, second], axis=1)
    order_keys = jax.random.split(key_order, fronts * 2 * BATCH * N_FRONT)
    ordering = jax.vmap(lambda single_key: jax.random.permutation(single_key, CT))(order_keys)
    ordering = ordering.reshape(fronts, 2, BATCH, N_FRONT, CT)
    slots = (omitted[..., None] + 1 + ordering) % PT
    return slots.reshape(2 * fronts, BATCH, N_FRONT, CT).astype(jnp.int32)


def draw_map_one(key, part):
    return draw_tile_maps(jax.random.fold_in(key, 37), N_LEAF // 2)


def draw_map_two(key, part):
    return draw_tile_maps(jax.random.fold_in(key, 41), N_LEAF // 4)


def place_ends(values, stream_key, low, top_value):
    longest = values.shape.index(max(values.shape))
    spots = []
    for shift in (0, 1):
        where = [jax.random.randint(jax.random.fold_in(stream_key, axis), (), 0, length) for axis, length in enumerate(values.shape)]
        where[longest] = (where[longest] + shift) % values.shape[longest]
        spots.append(tuple(where))
    return values.at[spots[0]].set(low).at[spots[1]].set(top_value)


def setup_inputs(seed: int = 0) -> dict:
    streams_of = jax.random.split(jax.random.key(seed), 8)
    child_update = draw_child_update(jax.random.fold_in(streams_of[7], 71), 0)
    sep_one = draw_sep_one(jax.random.fold_in(streams_of[7], 71), 0)
    sep_two = draw_sep_two(jax.random.fold_in(streams_of[7], 71), 0)
    map_one = draw_map_one(jax.random.fold_in(streams_of[7], 71), 0)
    map_two = draw_map_two(jax.random.fold_in(streams_of[7], 71), 0)
    mask_one = place_ends((jax.random.randint(streams_of[5], (N_LEAF // 2, BATCH, UT, ST), 0, 2) < 1).astype(jnp.int32), jax.random.fold_in(streams_of[5], 1), 0, 1)
    mask_two = place_ends((jax.random.randint(streams_of[6], (N_LEAF // 4, BATCH, UT, ST), 0, 2) < 1).astype(jnp.int32), jax.random.fold_in(streams_of[6], 1), 0, 1)
    return {"child_update": child_update, "sep_one": sep_one, "sep_two": sep_two, "map_one": map_one, "map_two": map_two, "mask_one": mask_one, "mask_two": mask_two}


def tile_targets(tile_map):
    slots = jnp.swapaxes(tile_map, -1, -2)
    offsets = jnp.arange(N_FRONT, dtype=jnp.int32)
    return (slots * N_FRONT + offsets).reshape(slots.shape[:-2] + (UT,)).astype(jnp.int32)

def extend_add(update, targets):
    within = jnp.arange(TILE, dtype=jnp.int32)
    positions = (targets[:, None] * TILE + within[None, :]).reshape(U).astype(jnp.int32)
    canvas = jnp.zeros((F, F), jnp.float32)
    return canvas.at[positions[:, None], positions[None, :]].add(update.astype(jnp.float32))

def assemble_front(first_child, second_child, first_targets, second_targets, initial, tile_mask):
    canvas = extend_add(first_child, first_targets) + extend_add(second_child, second_targets)
    mask_full = jnp.repeat(jnp.repeat(tile_mask.astype(jnp.float32), TILE, axis=0), TILE, axis=1)
    coupling = initial[S:].astype(jnp.float32) * mask_full
    columns = jnp.concatenate([initial[:S].astype(jnp.float32), coupling], axis=0)
    canvas = canvas.at[:, :S].add(columns)
    canvas = canvas.at[:S, S:].add(coupling.T)
    return canvas

def factor_front(canvas):
    lower_factor = jnp.linalg.cholesky(canvas[:S, :S])
    panel_full = lax.linalg.triangular_solve(lower_factor, canvas[S:, :S], left_side=False, lower=True, transpose_a=True)
    panel_round = panel_full.astype(jnp.bfloat16)
    trailing = canvas[S:, S:] - jnp.dot(panel_round.astype(jnp.float32), panel_round.T.astype(jnp.float32), preferred_element_type=jnp.float32)
    return (jnp.concatenate([lower_factor, panel_full], axis=0), trailing.astype(jnp.bfloat16))

def factor_level(children, targets, initial, tile_mask):
    fronts = initial.shape[0]
    count = fronts * BATCH
    inputs = (children[0::2].reshape(count, U, U), children[1::2].reshape(count, U, U), targets[0::2].reshape(count, UT), targets[1::2].reshape(count, UT), initial.reshape(count, F, S), tile_mask.reshape(count, UT, ST))

    def single(packed):
        return factor_front(assemble_front(*packed))
    factors, updates = lax.map(single, inputs)
    return (factors.reshape(fronts, BATCH, F, S), updates.reshape(fronts, BATCH, U, U))

def unpack_entries(entries, groups):
    fronts = N_LEAF // groups
    shaped = entries.reshape(fronts, groups, N_FRONT, BATCH, PT, TILE, S // groups)
    return jnp.transpose(shaped, (0, 3, 4, 2, 5, 1, 6)).reshape(fronts, BATCH, F, S)

def pack_columns(matrix, groups, row_tiles):
    fronts = matrix.shape[0]
    width = matrix.shape[-1]
    shaped = matrix.reshape(fronts, BATCH, row_tiles, N_FRONT, TILE, groups, width // groups)
    return jnp.transpose(shaped, (0, 5, 3, 1, 2, 4, 6)).reshape(fronts * groups, N_FRONT, BATCH, row_tiles, TILE, width // groups)

def reference(child_update, sep_one, sep_two, map_one, map_two, mask_one, mask_two):
    children = jnp.transpose(child_update, (0, 2, 3, 1, 4, 5)).reshape(N_LEAF, BATCH, U, U)
    target_one = tile_targets(map_one)
    target_two = tile_targets(map_two)
    orig_one = unpack_entries(sep_one, 2)
    orig_two = unpack_entries(sep_two, 4)
    factors_one, update_one = factor_level(children, target_one, orig_one, mask_one)
    factors_two, update_full = factor_level(update_one, target_two, orig_two, mask_two)
    factor_one = pack_columns(factors_one, 2, PT)
    factor_two = pack_columns(factors_two, 4, PT)
    update_two = pack_columns(update_full, 4, CT)
    return (factor_one, factor_two, update_two)
```

```python
import functools

import jax
import jax.numpy as jnp
from jax import lax
from jax.experimental import pallas as pl
from jax.experimental.pallas import tpu as pltpu
from jax.sharding import PartitionSpec as P

TILE = 256
ST = 4
UT = 12
S = 1024
U = 3072
C = 768
G = 128
F32 = jnp.float32
BF16 = jnp.bfloat16
VMEM_LIMIT = 60 * 1024 * 1024


def swapped(value, axis, apart):
    mask = 2**apart
    pairs = [(source, source ^ mask) for source in range(lax.axis_size(axis))]
    return lax.ppermute(value, axis, pairs)


def dot_nt(x, y):
    return lax.dot_general(x, y, (((1,), (1,)), ((), ())), preferred_element_type=F32)


def split(x):
    high = x.astype(BF16)
    return high, (x - high.astype(F32)).astype(BF16)


def left_parts(x):
    high, low = split(x)
    return jnp.concatenate([high, low, high], axis=1)


def right_parts(x):
    high, low = split(x)
    return jnp.concatenate([high, high, low], axis=1)


def source_of(map_ref, base, group, slot):
    first = map_ref[base + group * 3] == slot
    second = map_ref[base + group * 3 + 1] == slot
    third = map_ref[base + group * 3 + 2] == slot
    index = jnp.where(first, 0, jnp.where(second, 1, 2))
    live = jnp.logical_or(first, jnp.logical_or(second, third))
    return index, live


def invert_diagonal(block_ref, inverse_ref):
    sub = lax.broadcasted_iota(jnp.int32, (8, G), 0)
    lane = lax.broadcasted_iota(jnp.int32, (8, G), 1)
    slabs = G // 8
    rest = [block_ref[8 * r : 8 * r + 8, :] for r in range(slabs)]
    unit = [jnp.where(lane == sub + 8 * r, 1.0, 0.0).astype(F32) for r in range(slabs)]

    def lanes(v, c):
        return jnp.broadcast_to(v[:, c : c + 1], (8, G))

    def rows(v, i):
        return jnp.broadcast_to(v[i : i + 1, :], (8, G))

    for t in range(slabs):
        k = 8 * t
        cols = [lanes(rest[t], k + i) for i in range(8)]
        a = {(i, j): rows(cols[j], i) for j in range(8) for i in range(j, 8)}
        low = {}
        scale = []
        for i in range(8):
            scale.append(lax.rsqrt(a[i, i]))
            for j in range(i + 1, 8):
                low[j, i] = a[j, i] * scale[i]
            for j in range(i + 1, 8):
                for m in range(j, 8):
                    a[m, j] = a[m, j] - low[m, i] * low[j, i]

        def forward(pick):
            out = []
            for i in range(8):
                x = pick(i)
                for j in range(i):
                    x = x - low[i, j] * out[j]
                out.append(x * scale[i])
            return out

        upper = forward(lambda i: rows(rest[t], i))
        inv = forward(lambda i: rows(unit[t], i))
        packed = inv[0]
        for i in range(1, 8):
            packed = jnp.where(sub == i, inv[i], packed)
        inverse_ref[k : k + 8, :] = packed
        for r in range(t + 1, slabs):
            column = []
            for i in range(8):
                x = lanes(rest[r], k + i)
                for j in range(i):
                    x = x - column[j] * low[i, j]
                column.append(x * scale[i])
            for i in range(8):
                rest[r] = rest[r] - column[i] * upper[i]
                unit[r] = unit[r] - column[i] * inv[i]


def positions(level):
    leaf = lax.axis_index("leaf")
    group = lax.axis_index("front")
    child = leaf if level == 1 else leaf // 2
    half = child % 2
    return leaf, group, child, half


def initial_tile(own_ref, peer_ref, m, c, half):
    at = (m, slice(None), slice((c % 2) * TILE, (c % 2 + 1) * TILE))
    return jnp.where(half == c // 2, own_ref[at].astype(F32), peer_ref[at].astype(F32))


def pivot_kernel(level, map_ref, own_ref, peer_ref, init_own, init_peer, out_ref, tiles, sems):
    leaf, group, child, half = positions(level)
    places = []
    for side, ref in ((0, own_ref), (1, peer_ref)):
        base = (child ^ side) * 12
        row, row_live = source_of(map_ref, base, group, 0)
        for c in range(ST):
            col, col_live = source_of(map_ref, base, c, 0)
            start = pl.multiple_of((col * 4 + c) * TILE, TILE)
            copy = pltpu.make_async_copy(
                ref.at[row, :, pl.ds(start, TILE)], tiles.at[side, c], sems.at[side, c]
            )
            copy.start()
            places.append((copy, jnp.logical_and(row_live, col_live)))
    for copy, _ in places:
        copy.wait()
    for c in range(ST):
        own = jnp.where(places[c][1], tiles[0, c].astype(F32), 0.0)
        peer = jnp.where(places[ST + c][1], tiles[1, c].astype(F32), 0.0)
        init = initial_tile(init_own, init_peer, 0, c, half)
        out_ref[:, c * TILE : (c + 1) * TILE] = own + peer + init


def pivot_rows(level, tile_map, own, peer, init_own, init_peer):
    init_spec = pl.BlockSpec(memory_space=pltpu.VMEM)
    return pl.pallas_call(
        functools.partial(pivot_kernel, level),
        out_shape=jax.ShapeDtypeStruct((TILE, S), F32),
        in_specs=[
            pl.BlockSpec(memory_space=pltpu.SMEM),
            pl.BlockSpec(memory_space=pl.ANY),
            pl.BlockSpec(memory_space=pl.ANY),
            init_spec,
            init_spec,
        ],
        scratch_shapes=[
            pltpu.VMEM((2, ST, TILE, TILE), BF16),
            pltpu.SemaphoreType.DMA((2, ST)),
        ],
        name=f"pivot_{level}",
    )(tile_map, own, peer, init_own, init_peer)


def factor_kernel(
    level, map_ref, mask_ref, pivot_ref, own_ref, peer_ref, init_own, init_peer,
    factor_ref, panel_ref, a_ref, l_ref, xl_ref, xr_ref, inv_ref, tiles, sems
):
    leaf, group, child, half = positions(level)
    width = S // (2 * level)
    copies = []
    lives = {}
    for side, ref in ((0, own_ref), (1, peer_ref)):
        base = (child ^ side) * 12
        for m in range(1, 4):
            row, row_live = source_of(map_ref, base, group, m)
            for c in range(ST):
                col, col_live = source_of(map_ref, base, c, 0)
                start = pl.multiple_of((col * 4 + c) * TILE, TILE)
                slot = (m - 1) * ST + c
                copy = pltpu.make_async_copy(
                    ref.at[row, :, pl.ds(start, TILE)], tiles.at[side, slot], sems.at[side, slot]
                )
                copy.start()
                copies.append(copy)
                lives[side, slot] = jnp.logical_and(row_live, col_live)
    for t in range(ST):
        a_ref[t * TILE : (t + 1) * TILE, :] = pivot_ref[t]
    for copy in copies:
        copy.wait()
    for m in range(1, 4):
        for c in range(ST):
            slot = (m - 1) * ST + c
            own = jnp.where(lives[0, slot], tiles[0, slot].astype(F32), 0.0)
            peer = jnp.where(lives[1, slot], tiles[1, slot].astype(F32), 0.0)
            keep = mask_ref[((child // 2) * UT + (m - 1) * 4 + group) * ST + c].astype(F32)
            init = initial_tile(init_own, init_peer, m, c, half) * keep
            a_ref[S + (m - 1) * TILE : S + m * TILE, c * TILE : (c + 1) * TILE] = own + peer + init

    def step(g, _):
        cols = pl.ds(pl.multiple_of(g * G, G), G)
        invert_diagonal(a_ref.at[cols, cols], inv_ref)
        inverse = right_parts(inv_ref[...])

        def panel(low, high):
            x = dot_nt(left_parts(a_ref[low:high, cols]), inverse)
            l_ref[low:high, cols] = x
            xl_ref[low:high, :] = left_parts(x)
            if low < S:
                xr_ref[low:high, :] = right_parts(x)

        @pl.when(g < 4)
        def _():
            panel(0, S // 2)

        panel(S // 2, S)
        panel(S, S + C)
        for block in range(ST):

            @pl.when(g < 2 * block + 1)
            def _():
                there = slice(block * TILE, (block + 1) * TILE)
                a_ref[block * TILE :, there] -= dot_nt(xl_ref[block * TILE :, :], xr_ref[there, :])

        return 0

    lax.fori_loop(0, S // G, step, 0)
    part = pl.ds(pl.multiple_of((leaf % (2 * level)) * width, width), width)
    row = lax.broadcasted_iota(jnp.int32, (TILE, width), 0) + group * TILE
    col = lax.broadcasted_iota(jnp.int32, (TILE, width), 1) + (leaf % (2 * level)) * width
    own_rows = l_ref[pl.ds(pl.multiple_of(group * TILE, TILE), TILE), part]
    factor_ref[0] = jnp.where(row >= col, own_rows, 0.0)
    for m in range(1, 4):
        factor_ref[m] = l_ref[S + (m - 1) * TILE : S + m * TILE, part]
    panel_ref[...] = l_ref[S:, :].astype(BF16)


def factor_rows(level, tile_map, tile_mask, pivot, own, peer, init_own, init_peer):
    width = S // (2 * level)
    vmem = pl.BlockSpec(memory_space=pltpu.VMEM)
    smem = pl.BlockSpec(memory_space=pltpu.SMEM)
    hbm = pl.BlockSpec(memory_space=pl.ANY)
    return pl.pallas_call(
        functools.partial(factor_kernel, level),
        out_shape=[
            jax.ShapeDtypeStruct((4, TILE, width), F32),
            jax.ShapeDtypeStruct((C, S), BF16),
        ],
        in_specs=[smem, smem, vmem, hbm, hbm, vmem, vmem],
        scratch_shapes=[
            pltpu.VMEM((S + C, S), F32),
            pltpu.VMEM((S + C, S), F32),
            pltpu.VMEM((S + C, 3 * G), BF16),
            pltpu.VMEM((S, 3 * G), BF16),
            pltpu.VMEM((G, G), F32),
            pltpu.VMEM((2, 12, TILE, TILE), BF16),
            pltpu.SemaphoreType.DMA((2, 12)),
        ],
        compiler_params=pltpu.CompilerParams(vmem_limit_bytes=VMEM_LIMIT),
        name=f"factor_{level}",
    )(tile_map, tile_mask, pivot, own, peer, init_own, init_peer)


def update_kernel(level, map_ref, x_ref, y_ref, *rest):
    tiles, out_ref = rest[:6], rest[6]
    leaf, group, child, half = positions(level)
    v = pl.program_id(0) + (0 if level == 1 else (leaf % 4) * 3)
    product = dot_nt(x_ref[...], y_ref[0])
    for m in range(1, 4):
        total = -product[(m - 1) * TILE : m * TILE, :]
        for side in (0, 1):
            base = (child ^ side) * 12
            _, row_live = source_of(map_ref, base, group, m)
            _, col_live = source_of(map_ref, base, v % 4, 1 + v // 4)
            live = jnp.logical_and(row_live, col_live)
            total = total + jnp.where(live, tiles[2 * (m - 1) + side][0].astype(F32), 0.0)
        out_ref[m - 1] = total.astype(BF16)


def update_rows(level, tile_map, panel, panels, own, peer):
    def offset():
        return 0 if level == 1 else (lax.axis_index("leaf") % 4) * 3

    place = jnp.stack([lax.axis_index("leaf"), lax.axis_index("front")]).astype(jnp.int32)

    def start(v, place_ref):
        return v + (0 if level == 1 else (place_ref[0] % 4) * 3)

    def panel_block(v, place_ref, map_ref):
        at = start(v, place_ref)
        return (at % 4, at // 4, 0)

    def tile_block(m, side, v, place_ref, map_ref):
        at = start(v, place_ref)
        child = place_ref[0] if level == 1 else place_ref[0] // 2
        base = (child ^ side) * 12
        row, _ = source_of(map_ref, base, place_ref[1], m)
        col, _ = source_of(map_ref, base, at % 4, 1 + at // 4)
        return (row, 0, col * 4 + at % 4)

    def kernel(place_ref, map_ref, *refs):
        update_kernel(level, map_ref, *refs)

    count = 12 if level == 1 else 3
    tile_specs = [
        pl.BlockSpec((1, TILE, TILE), functools.partial(tile_block, m, side))
        for m in range(1, 4)
        for side in (0, 1)
    ]
    return pl.pallas_call(
        kernel,
        out_shape=jax.ShapeDtypeStruct((3, TILE, TILE * count), BF16),
        grid_spec=pltpu.PrefetchScalarGridSpec(
            num_scalar_prefetch=2,
            grid=(count,),
            in_specs=[
                pl.BlockSpec((C, S), lambda v, p, q: (0, 0)),
                pl.BlockSpec((1, TILE, S), panel_block),
                *tile_specs,
            ],
            out_specs=pl.BlockSpec((3, TILE, TILE), lambda v, p, q: (0, 0, v)),
        ),
        compiler_params=pltpu.CompilerParams(vmem_limit_bytes=VMEM_LIMIT),
        name=f"update_{level}",
    )(place, tile_map, panel, panels, *([own, peer] * 3))


def join_halves(mine, other, position):
    lower_first = jnp.concatenate([mine, other], axis=-1)
    upper_first = jnp.concatenate([other, mine], axis=-1)
    return jnp.where(position == 0, lower_first, upper_first)


def level_step(level, tile_map, tile_mask, own, peer, init_own, init_peer):
    pivot = pivot_rows(level, tile_map, own, peer, init_own, init_peer)
    pivots = lax.all_gather(pivot, "front", axis=0)
    factor, panel = factor_rows(level, tile_map, tile_mask, pivots, own, peer, init_own, init_peer)
    panels = lax.all_gather(panel, "front", axis=0)
    update = update_rows(level, tile_map, panel, panels, own, peer)
    return factor, update


def body(child_update, sep_one, sep_two, map_one, map_two, mask_one, mask_two):
    leaf = lax.axis_index("leaf")
    own = child_update[0, 0, 0]
    init_own = sep_one[0, 0, 0]
    quarter = sep_two[0, 0, 0]
    peer, init_peer, quarter_peer = swapped((own, init_own, quarter), "leaf", 0)
    factor_one, update_one = level_step(
        1, map_one.reshape(-1), mask_one.reshape(-1), own, peer, init_own, init_peer
    )
    near = join_halves(quarter, quarter_peer, leaf % 2)
    far_update, far = swapped((update_one, near), "leaf", 1)
    factor_two, update_two = level_step(
        2, map_two.reshape(-1), mask_two.reshape(-1), update_one, far_update, near, far
    )
    return (factor_one[None, None, None], factor_two[None, None, None], update_two[None, None, None])


def solution(mesh):
    split_spec = P("leaf", "front", None, None, None, None)
    return jax.shard_map(
        body,
        mesh=mesh,
        in_specs=(split_spec, split_spec, split_spec, P(), P(), P(), P()),
        out_specs=(split_spec, split_spec, split_spec),
        check_vma=False,
    )
```

```python
import functools

import jax
import jax.numpy as jnp
from jax import lax
from jax.experimental import pallas as pl
from jax.experimental.pallas import tpu as pltpu
from jax.sharding import PartitionSpec as P

TILE = 256
ST = 4
UT = 12
RING = 4
S = 1024
U = 3072
C = 768
G = 128
F32 = jnp.float32
BF16 = jnp.bfloat16
VMEM_LIMIT = 60 * 1024 * 1024


def swapped(value, axis, apart):
    mask = 2**apart
    pairs = [(source, source ^ mask) for source in range(lax.axis_size(axis))]
    return lax.ppermute(value, axis, pairs)


def dot_nt(x, y):
    return lax.dot_general(x, y, (((1,), (1,)), ((), ())), preferred_element_type=F32)


def split(x):
    high = x.astype(BF16)
    return high, (x - high.astype(F32)).astype(BF16)


def left_parts(x):
    high, low = split(x)
    return jnp.concatenate([high, low, high], axis=1)


def right_parts(x):
    high, low = split(x)
    return jnp.concatenate([high, high, low], axis=1)


def source_of(map_ref, base, group, slot):
    first = map_ref[base + group * 3] == slot
    second = map_ref[base + group * 3 + 1] == slot
    third = map_ref[base + group * 3 + 2] == slot
    index = jnp.where(first, 0, jnp.where(second, 1, 2))
    live = jnp.logical_or(first, jnp.logical_or(second, third))
    return index, live


def invert_diagonal(block_ref, inverse_ref):
    sub = lax.broadcasted_iota(jnp.int32, (8, G), 0)
    lane = lax.broadcasted_iota(jnp.int32, (8, G), 1)
    slabs = G // 8
    rest = [block_ref[8 * r : 8 * r + 8, :] for r in range(slabs)]
    unit = [jnp.where(lane == sub + 8 * r, 1.0, 0.0).astype(F32) for r in range(slabs)]

    def lanes(v, c):
        return jnp.broadcast_to(v[:, c : c + 1], (8, G))

    def rows(v, i):
        return jnp.broadcast_to(v[i : i + 1, :], (8, G))

    for t in range(slabs):
        k = 8 * t
        cols = [lanes(rest[t], k + i) for i in range(8)]
        a = {(i, j): rows(cols[j], i) for j in range(8) for i in range(j, 8)}
        low = {}
        scale = []
        for i in range(8):
            scale.append(lax.rsqrt(a[i, i]))
            for j in range(i + 1, 8):
                low[j, i] = a[j, i] * scale[i]
            for j in range(i + 1, 8):
                for m in range(j, 8):
                    a[m, j] = a[m, j] - low[m, i] * low[j, i]

        def forward(pick):
            out = []
            for i in range(8):
                x = pick(i)
                for j in range(i):
                    x = x - low[i, j] * out[j]
                out.append(x * scale[i])
            return out

        upper = forward(lambda i: rows(rest[t], i))
        inv = forward(lambda i: rows(unit[t], i))
        packed = inv[0]
        for i in range(1, 8):
            packed = jnp.where(sub == i, inv[i], packed)
        inverse_ref[k : k + 8, :] = packed
        for r in range(t + 1, slabs):
            column = []
            for i in range(8):
                x = lanes(rest[r], k + i)
                for j in range(i):
                    x = x - column[j] * low[i, j]
                column.append(x * scale[i])
            for i in range(8):
                rest[r] = rest[r] - column[i] * upper[i]
                unit[r] = unit[r] - column[i] * inv[i]


def place():
    return lax.axis_index("leaf"), lax.axis_index("front")


def spread_kernel(map_ref, child_ref, out_ref, sems):
    leaf, group = place()
    copies = []
    for m in range(4):
        row, row_live = source_of(map_ref, leaf * UT, group, m)
        for c in range(ST):
            col, col_live = source_of(map_ref, leaf * UT, c, 0)
            start = pl.multiple_of((col * 4 + c) * TILE, TILE)
            there = slice(c * TILE, (c + 1) * TILE)
            copy = pltpu.make_async_copy(
                child_ref.at[row, :, pl.ds(start, TILE)], out_ref.at[m, :, there], sems.at[m, c]
            )
            copy.start()
            copies.append((copy, m, there, jnp.logical_and(row_live, col_live)))
    for copy, m, there, live in copies:
        copy.wait()

        @pl.when(jnp.logical_not(live))
        def _():
            out_ref[m, :, there] = jnp.zeros((TILE, TILE), BF16)


def spread(tile_map, child):
    return pl.pallas_call(
        spread_kernel,
        out_shape=jax.ShapeDtypeStruct((4, TILE, S), BF16),
        in_specs=[pl.BlockSpec(memory_space=pltpu.SMEM), pl.BlockSpec(memory_space=pl.ANY)],
        scratch_shapes=[pltpu.SemaphoreType.DMA((4, ST))],
        name="spread",
    )(tile_map, child)


def initial_kernel(level, mask_ref, own_ref, peer_ref, out_ref):
    leaf, group = place()
    front = leaf // (2 * level)
    half = (leaf // level) % 2
    for m in range(4):
        for c in range(ST):
            at = (m, slice(None), slice((c % 2) * TILE, (c % 2 + 1) * TILE))
            value = jnp.where(half == c // 2, own_ref[at].astype(F32), peer_ref[at].astype(F32))
            if m > 0:
                value = value * mask_ref[(front * UT + (m - 1) * 4 + group) * ST + c].astype(F32)
            out_ref[m, :, c * TILE : (c + 1) * TILE] = value.astype(BF16)


def initial(level, tile_mask, own, peer):
    vmem = pl.BlockSpec(memory_space=pltpu.VMEM)
    return pl.pallas_call(
        functools.partial(initial_kernel, level),
        out_shape=jax.ShapeDtypeStruct((4, TILE, S), BF16),
        in_specs=[pl.BlockSpec(memory_space=pltpu.SMEM), vmem, vmem],
        name=f"initial_{level}",
    )(tile_mask, own, peer)


def meet(devices):
    barrier = pltpu.get_barrier_semaphore()
    for device in devices:
        pl.semaphore_signal(
            barrier, inc=1, device_id=device, device_id_type=pl.DeviceIdType.MESH
        )
    pl.semaphore_wait(barrier, len(devices))


def remote(source, target, sems, slot, device):
    return pltpu.make_async_remote_copy(
        src_ref=source,
        dst_ref=target,
        send_sem=sems.at[0, slot],
        recv_sem=sems.at[1, slot],
        device_id=device,
        device_id_type=pl.DeviceIdType.MESH,
    )


def ring(buf, low, size, sems, slot, sibling):
    leaf, me = place()
    right, left, across = lax.rem(me + 1, RING), lax.rem(me + 3, RING), lax.rem(me + 2, RING)
    to_right, to_left = {"front": right}, {"front": left}
    part = size // 2
    first, second, whole = pl.ds(low, part), pl.ds(low + part, part), pl.ds(low, size)

    def send(source, rows, device, k):
        copy = remote(buf.at[source, rows], buf.at[source, rows], sems, slot + k, device)
        copy.start()
        return copy

    right_1 = send(me, first, to_right, 0)
    left_1 = send(me, second, to_left, 1)
    right_2 = send(me, second, to_right, 2)
    left_2 = send(me, first, to_left, 3)
    others = []
    if sibling is not None:
        others.append(send(me, whole, sibling, 6))
    right_1.wait_recv()
    right_3 = send(left, first, to_right, 4)
    left_1.wait_recv()
    left_3 = send(right, second, to_left, 5)
    right_2.wait_recv()
    if sibling is not None:
        others.append(send(left, whole, sibling, 7))
    left_2.wait_recv()
    if sibling is not None:
        others.append(send(right, whole, sibling, 8))
    right_3.wait_recv()
    left_3.wait_recv()
    if sibling is not None:
        others.append(send(across, whole, sibling, 9))
    for copy in others:
        copy.wait_recv()
    for copy in [right_1, left_1, right_2, left_2, right_3, left_3, *others]:
        copy.wait_send()


def neighbours():
    _, me = place()
    return [{"front": lax.rem(me + 1, RING)}, {"front": lax.rem(me + 3, RING)}]


def exchange_kernel(
    level, near_ref, init_ref, pivots_ref, far_ref, near_buf, init_buf, far_buf, sems, local_sems
):
    leaf, me = place()
    core = lax.rem(leaf, 2)
    sibling = {"leaf": leaf + 1 - 2 * core}
    bit = lax.rem(leaf // level, 2)
    partner = {"leaf": leaf + level * (1 - 2 * bit)}
    meet(neighbours() + [sibling] + ([partner] if level == 2 else []))
    half = TILE // 2
    low = pl.multiple_of(core * half, half)
    mine = pl.ds(low, half)
    theirs = mine if level == 2 else pl.ds(pl.multiple_of(half - low, half), half)
    pivot_copy = remote(near_ref.at[0, theirs], far_buf, sems, 10, partner)
    pivot_copy.start()
    if level == 1:
        coupling = remote(near_ref.at[pl.ds(1, 3)], far_ref, sems, 11, partner)
    else:
        coupling = remote(near_ref.at[pl.ds(1, 3), mine], far_ref.at[:, mine], sems, 11, partner)
    coupling.start()
    near_copy = pltpu.make_async_copy(near_ref.at[0, mine], near_buf, local_sems.at[0])
    init_copy = pltpu.make_async_copy(init_ref.at[0, mine], init_buf, local_sems.at[1])
    near_copy.start()
    init_copy.start()
    near_copy.wait()
    init_copy.wait()
    pivot_copy.wait_recv()
    pivots_ref[me, mine] = (
        near_buf[...].astype(F32) + far_buf[...].astype(F32) + init_buf[...].astype(F32)
    )
    ring(pivots_ref, low, half, sems, 0, sibling)
    coupling.wait_recv()
    if level == 2:
        onward = remote(far_ref.at[:, mine], far_ref.at[:, mine], sems, 12, sibling)
        onward.start()
        onward.wait()
    pivot_copy.wait_send()
    coupling.wait_send()


def exchange(level, near, init):
    hbm = pl.BlockSpec(memory_space=pl.ANY)
    half = TILE // 2
    return pl.pallas_call(
        functools.partial(exchange_kernel, level),
        out_shape=[
            jax.ShapeDtypeStruct((RING, TILE, S), F32),
            jax.ShapeDtypeStruct((3, TILE, S), BF16),
        ],
        in_specs=[hbm, hbm],
        out_specs=[pl.BlockSpec(memory_space=pltpu.VMEM), hbm],
        scratch_shapes=[
            pltpu.VMEM((half, S), BF16),
            pltpu.VMEM((half, S), BF16),
            pltpu.VMEM((half, S), BF16),
            pltpu.SemaphoreType.DMA((2, 13)),
            pltpu.SemaphoreType.DMA((2,)),
        ],
        compiler_params=pltpu.CompilerParams(
            collective_id=level, has_side_effects=True, vmem_limit_bytes=VMEM_LIMIT
        ),
        name=f"exchange_{level}",
    )(near, init)


def gather_one_kernel(panel_ref, out_ref, sems, local_sem):
    leaf, me = place()
    core = lax.rem(leaf, 2)
    sibling = {"leaf": leaf + 1 - 2 * core}
    meet(neighbours() + [sibling])
    half = C // 2
    mine = pl.ds(pl.multiple_of(core * half, half), half)
    copy = pltpu.make_async_copy(panel_ref.at[mine], out_ref.at[me, mine], local_sem)
    copy.start()
    copy.wait()
    ring(out_ref, pl.multiple_of(core * half, half), half, sems, 0, sibling)


def gather_two_kernel(panel_ref, out_ref, sems, local_sem):
    leaf, me = place()
    meet(neighbours())
    quarter = lax.rem(leaf, 4)
    column = lax.rem(me + quarter, RING)
    tile = lax.min((3 * quarter + column) // 4, 2)
    rows = pl.ds(pl.multiple_of(tile * TILE, TILE), TILE)
    copy = pltpu.make_async_copy(panel_ref.at[rows], out_ref.at[me], local_sem)
    copy.start()
    copy.wait()
    ring(out_ref, 0, TILE, sems, 0, None)


def gather(level, panel):
    hbm = pl.BlockSpec(memory_space=pl.ANY)
    kernel = gather_one_kernel if level == 1 else gather_two_kernel
    return pl.pallas_call(
        kernel,
        out_shape=jax.ShapeDtypeStruct((RING, C if level == 1 else TILE, S), BF16),
        in_specs=[hbm],
        out_specs=hbm,
        scratch_shapes=[
            pltpu.SemaphoreType.DMA((2, 10 if level == 1 else 6)),
            pltpu.SemaphoreType.DMA,
        ],
        compiler_params=pltpu.CompilerParams(
            collective_id=2 + level, has_side_effects=True, vmem_limit_bytes=VMEM_LIMIT
        ),
        name=f"gather_{level}",
    )(panel)


def factor_kernel(
    level, pivot_ref, near_ref, far_ref, init_ref,
    factor_ref, panel_ref, a_ref, l_ref, xl_ref, xr_ref, inv_ref, parts, sems
):
    leaf, group = place()
    width = S // (2 * level)
    pivots = []
    for t in range(RING):
        copy = pltpu.make_async_copy(
            pivot_ref.at[t], a_ref.at[pl.ds(t * TILE, TILE)], sems.at[3 + t]
        )
        copy.start()
        pivots.append(copy)
    sides = [near_ref.at[pl.ds(1, 3)], far_ref, init_ref.at[pl.ds(1, 3)]]
    copies = []
    for k, side in enumerate(sides):
        copy = pltpu.make_async_copy(side, parts.at[k], sems.at[k])
        copy.start()
        copies.append(copy)
    for copy in pivots + copies:
        copy.wait()
    for m in range(3):
        a_ref[S + m * TILE : S + (m + 1) * TILE, :] = (
            parts[0, m].astype(F32) + parts[1, m].astype(F32) + parts[2, m].astype(F32)
        )

    def step(g, _):
        cols = pl.ds(pl.multiple_of(g * G, G), G)
        invert_diagonal(a_ref.at[cols, cols], inv_ref)
        inverse = right_parts(inv_ref[...])

        def panel(low, high):
            x = dot_nt(left_parts(a_ref[low:high, cols]), inverse)
            l_ref[low:high, cols] = x
            xl_ref[low:high, :] = left_parts(x)
            if low < S:
                xr_ref[low:high, :] = right_parts(x)

        @pl.when(g < 4)
        def _():
            panel(0, S // 2)

        panel(S // 2, S)
        panel(S, S + C)
        for block in range(ST):

            @pl.when(g < 2 * block + 1)
            def _():
                there = slice(block * TILE, (block + 1) * TILE)
                a_ref[block * TILE :, there] -= dot_nt(xl_ref[block * TILE :, :], xr_ref[there, :])

        return 0

    lax.fori_loop(0, S // G, step, 0)
    part = pl.ds(pl.multiple_of((leaf % (2 * level)) * width, width), width)
    row = lax.broadcasted_iota(jnp.int32, (TILE, width), 0) + group * TILE
    col = lax.broadcasted_iota(jnp.int32, (TILE, width), 1) + (leaf % (2 * level)) * width
    own_rows = l_ref[pl.ds(pl.multiple_of(group * TILE, TILE), TILE), part]
    factor_ref[0] = jnp.where(row >= col, own_rows, 0.0)
    for m in range(1, 4):
        factor_ref[m] = l_ref[S + (m - 1) * TILE : S + m * TILE, part]
    panel_ref[...] = l_ref[S:, :].astype(BF16)


def factor_rows(level, pivots, near, far, init):
    width = S // (2 * level)
    hbm = pl.BlockSpec(memory_space=pl.ANY)
    return pl.pallas_call(
        functools.partial(factor_kernel, level),
        out_shape=[
            jax.ShapeDtypeStruct((4, TILE, width), F32),
            jax.ShapeDtypeStruct((C, S), BF16),
        ],
        in_specs=[hbm] * 4,
        scratch_shapes=[
            pltpu.VMEM((S + C, S), F32),
            pltpu.VMEM((S + C, S), F32),
            pltpu.VMEM((S + C, 3 * G), BF16),
            pltpu.VMEM((S, 3 * G), BF16),
            pltpu.VMEM((G, G), F32),
            pltpu.VMEM((3, 3, TILE, S), BF16),
            pltpu.SemaphoreType.DMA((7,)),
        ],
        compiler_params=pltpu.CompilerParams(vmem_limit_bytes=VMEM_LIMIT),
        cost_estimate=pl.CostEstimate(
            flops=50_000_000_000, bytes_accessed=20_000_000, transcendentals=0
        ),
        name=f"factor_{level}",
    )(pivots, near, far, init)


def update_one_rows(map_one, map_two, panel, panels, own, peer):
    here = jnp.stack(place()).astype(jnp.int32)

    def column(i, here_ref, two_ref):
        quarter = here_ref[0] % 4
        across = (quarter + 2) % 4
        t = jnp.where(i < 4, i, jnp.where(i < 7, 3 * quarter + i, 3 * across + i - 3))
        tile, live = source_of(two_ref, (here_ref[0] // 2) * UT, t % 4, t // 4)
        return t % 4, tile, live

    def panel_block(i, here_ref, one_ref, two_ref):
        other, tile, _ = column(i, here_ref, two_ref)
        return (other, tile, 0)

    def tile_block(s, side, i, here_ref, one_ref, two_ref):
        other, tile, _ = column(i, here_ref, two_ref)
        base = (here_ref[0] ^ side) * UT
        row, _ = source_of(one_ref, base, here_ref[1], 1 + s)
        col, _ = source_of(one_ref, base, other, 1 + tile)
        return (row, 0, col * 4 + other)

    def kernel(here_ref, one_ref, two_ref, x_ref, y_ref, *refs):
        tiles, pivot_out, near_out, far_out, total_ref = refs[:6], *refs[6:]
        i = pl.program_id(0)
        other, tile, col_live = column(i, here_ref, two_ref)
        product = dot_nt(x_ref[...], y_ref[0])
        for s in range(3):
            total = -product[s * TILE : (s + 1) * TILE, :]
            for side in (0, 1):
                base = (here_ref[0] ^ side) * UT
                _, live_row = source_of(one_ref, base, here_ref[1], 1 + s)
                _, live_col = source_of(one_ref, base, other, 1 + tile)
                live = jnp.logical_and(live_row, live_col)
                total = total + jnp.where(live, tiles[2 * s + side][0].astype(F32), 0.0)
            total_ref[s] = total.astype(BF16)

        def target(m):
            row, row_live = source_of(two_ref, (here_ref[0] // 2) * UT, here_ref[1], m)
            live = jnp.logical_and(row_live, col_live)
            return jnp.where(live, total_ref[row].astype(F32), 0.0).astype(BF16)

        @pl.when(i < 4)
        def _():
            for m in range(4):
                pivot_out[m] = target(m)

        @pl.when(jnp.logical_and(i >= 4, i < 7))
        def _():
            for m in range(1, 4):
                near_out[m - 1] = target(m)

        @pl.when(i >= 7)
        def _():
            for m in range(1, 4):
                far_out[m - 1] = target(m)

    return pl.pallas_call(
        kernel,
        out_shape=[
            jax.ShapeDtypeStruct((4, TILE, S), BF16),
            jax.ShapeDtypeStruct((3, TILE, C), BF16),
            jax.ShapeDtypeStruct((3, TILE, C), BF16),
        ],
        grid_spec=pltpu.PrefetchScalarGridSpec(
            num_scalar_prefetch=3,
            grid=(10,),
            in_specs=[
                pl.BlockSpec((C, S), lambda i, *_: (0, 0)),
                pl.BlockSpec((1, TILE, S), panel_block),
                *[
                    pl.BlockSpec((1, TILE, TILE), functools.partial(tile_block, s, side))
                    for s in range(3)
                    for side in (0, 1)
                ],
            ],
            out_specs=[
                pl.BlockSpec((4, TILE, TILE), lambda i, *_: (0, 0, jnp.minimum(i, 3))),
                pl.BlockSpec((3, TILE, TILE), lambda i, *_: (0, 0, jnp.clip(i - 4, 0, 2))),
                pl.BlockSpec((3, TILE, TILE), lambda i, *_: (0, 0, jnp.clip(i - 7, 0, 2))),
            ],
            scratch_shapes=[pltpu.VMEM((3, TILE, TILE), BF16)],
        ),
        compiler_params=pltpu.CompilerParams(vmem_limit_bytes=VMEM_LIMIT),
        name="update_1",
    )(here, map_one, map_two, panel, panels, *([own, peer] * 3))


def update_two_kernel(x_ref, y_ref, near_ref, far_ref, out_ref):
    leaf, _ = place()
    quarter = lax.rem(leaf, 4)
    for i in range(3):
        there = slice(i * TILE, (i + 1) * TILE)
        product = dot_nt(x_ref[...], y_ref[lax.rem(3 * quarter + i, RING)])
        for m in range(3):
            front = near_ref[m, :, there].astype(F32) + far_ref[m, :, there].astype(F32)
            out_ref[m, :, there] = (front - product[m * TILE : (m + 1) * TILE, :]).astype(BF16)


def update_two_rows(panel, panels, near, far):
    vmem = pl.BlockSpec(memory_space=pltpu.VMEM)
    return pl.pallas_call(
        update_two_kernel,
        out_shape=jax.ShapeDtypeStruct((3, TILE, C), BF16),
        in_specs=[vmem] * 4,
        compiler_params=pltpu.CompilerParams(vmem_limit_bytes=VMEM_LIMIT),
        name="update_2",
    )(panel, panels, near, far)


def join_halves(mine, other, position):
    lower_first = jnp.concatenate([mine, other], axis=-1)
    upper_first = jnp.concatenate([other, mine], axis=-1)
    return jnp.where(position == 0, lower_first, upper_first)


def body(child_update, sep_one, sep_two, map_one, map_two, mask_one, mask_two):
    leaf = lax.axis_index("leaf")
    own = child_update[0, 0, 0]
    entries = sep_one[0, 0, 0]
    quarter = sep_two[0, 0, 0]
    map_one, map_two = map_one.reshape(-1), map_two.reshape(-1)
    entries_peer, quarter_peer, peer = swapped((entries, quarter, own), "leaf", 0)
    near = spread(map_one, own)
    init = initial(1, mask_one.reshape(-1), entries, entries_peer)
    half = join_halves(quarter, quarter_peer, leaf % 2)
    pivots, far = exchange(1, near, init)
    half_far = swapped(half, "leaf", 1)
    factor_one, panel = factor_rows(1, pivots, near, far, init)
    panel, half, half_far = lax.optimization_barrier((panel, half, half_far))
    init_two = initial(2, mask_two.reshape(-1), half, half_far)
    panels = gather(1, panel)
    near, rest_near, rest_far = update_one_rows(map_one, map_two, panel, panels, own, peer)
    pivots, far = exchange(2, near, init_two)
    pivots, rest_far = lax.optimization_barrier((pivots, rest_far))
    rest_far = swapped(rest_far, "leaf", 1)
    factor_two, panel = factor_rows(2, pivots, near, far, init_two)
    panel, rest_far = lax.optimization_barrier((panel, rest_far))
    panels = gather(2, panel)
    update_two = update_two_rows(panel, panels, rest_near, rest_far)
    return (factor_one[None, None, None], factor_two[None, None, None], update_two[None, None, None])


def solution(mesh):
    split_spec = P("leaf", "front", None, None, None, None)
    return jax.shard_map(
        body,
        mesh=mesh,
        in_specs=(split_spec, split_spec, split_spec, P(), P(), P(), P()),
        out_specs=(split_spec, split_spec, split_spec),
        check_vma=False,
    )
```

```python
import functools

import jax
import jax.numpy as jnp
from jax import lax
from jax.experimental import pallas as pl
from jax.experimental.pallas import tpu as pltpu
from jax.sharding import PartitionSpec as P

TILE = 256
ST = 4
UT = 12
RING = 4
S = 1024
U = 3072
C = 768
G = 128
F32 = jnp.float32
BF16 = jnp.bfloat16
VMEM_LIMIT = 60 * 1024 * 1024


def swapped(value, axis, apart):
    mask = 2**apart
    pairs = [(source, source ^ mask) for source in range(lax.axis_size(axis))]
    return lax.ppermute(value, axis, pairs)


def dot_nt(x, y):
    return lax.dot_general(x, y, (((1,), (1,)), ((), ())), preferred_element_type=F32)


def split(x):
    high = x.astype(BF16)
    return high, (x - high.astype(F32)).astype(BF16)


def left_parts(x):
    high, low = split(x)
    return jnp.concatenate([high, low, high], axis=1)


def right_parts(x):
    high, low = split(x)
    return jnp.concatenate([high, high, low], axis=1)


def source_of(map_ref, base, group, slot):
    first = map_ref[base + group * 3] == slot
    second = map_ref[base + group * 3 + 1] == slot
    third = map_ref[base + group * 3 + 2] == slot
    index = jnp.where(first, 0, jnp.where(second, 1, 2))
    live = jnp.logical_or(first, jnp.logical_or(second, third))
    return index, live


def invert_diagonal(block_ref, inverse_ref):
    sub = lax.broadcasted_iota(jnp.int32, (8, G), 0)
    lane = lax.broadcasted_iota(jnp.int32, (8, G), 1)
    slabs = G // 8
    rest = [block_ref[8 * r : 8 * r + 8, :] for r in range(slabs)]
    unit = [jnp.where(lane == sub + 8 * r, 1.0, 0.0).astype(F32) for r in range(slabs)]

    def lanes(v, c):
        return jnp.broadcast_to(v[:, c : c + 1], (8, G))

    def rows(v, i):
        return jnp.broadcast_to(v[i : i + 1, :], (8, G))

    for t in range(slabs):
        k = 8 * t
        cols = [lanes(rest[t], k + i) for i in range(8)]
        a = {(i, j): rows(cols[j], i) for j in range(8) for i in range(j, 8)}
        low = {}
        scale = []
        for i in range(8):
            scale.append(lax.rsqrt(a[i, i]))
            for j in range(i + 1, 8):
                low[j, i] = a[j, i] * scale[i]
            for j in range(i + 1, 8):
                for m in range(j, 8):
                    a[m, j] = a[m, j] - low[m, i] * low[j, i]

        def forward(pick):
            out = []
            for i in range(8):
                x = pick(i)
                for j in range(i):
                    x = x - low[i, j] * out[j]
                out.append(x * scale[i])
            return out

        upper = forward(lambda i: rows(rest[t], i))
        inv = forward(lambda i: rows(unit[t], i))
        packed = inv[0]
        for i in range(1, 8):
            packed = jnp.where(sub == i, inv[i], packed)
        inverse_ref[k : k + 8, :] = packed
        for r in range(t + 1, slabs):
            column = []
            for i in range(8):
                x = lanes(rest[r], k + i)
                for j in range(i):
                    x = x - column[j] * low[i, j]
                column.append(x * scale[i])
            for i in range(8):
                rest[r] = rest[r] - column[i] * upper[i]
                unit[r] = unit[r] - column[i] * inv[i]


def place():
    return lax.axis_index("leaf"), lax.axis_index("front")


def spread_kernel(map_ref, child_ref, out_ref, sems):
    leaf, group = place()
    copies = []
    for m in range(4):
        row, row_live = source_of(map_ref, leaf * UT, group, m)
        for c in range(ST):
            col, col_live = source_of(map_ref, leaf * UT, c, 0)
            start = pl.multiple_of((col * 4 + c) * TILE, TILE)
            there = slice(c * TILE, (c + 1) * TILE)
            copy = pltpu.make_async_copy(
                child_ref.at[row, :, pl.ds(start, TILE)], out_ref.at[m, :, there], sems.at[m, c]
            )
            copy.start()
            copies.append((copy, m, there, jnp.logical_and(row_live, col_live)))
    for copy, m, there, live in copies:
        copy.wait()

        @pl.when(jnp.logical_not(live))
        def _():
            out_ref[m, :, there] = jnp.zeros((TILE, TILE), BF16)


def spread(tile_map, child):
    return pl.pallas_call(
        spread_kernel,
        out_shape=jax.ShapeDtypeStruct((4, TILE, S), BF16),
        in_specs=[pl.BlockSpec(memory_space=pltpu.SMEM), pl.BlockSpec(memory_space=pl.ANY)],
        scratch_shapes=[pltpu.SemaphoreType.DMA((4, ST))],
        name="spread",
    )(tile_map, child)


def initial_kernel(level, mask_ref, own_ref, peer_ref, out_ref):
    leaf, group = place()
    front = leaf // (2 * level)
    half = (leaf // level) % 2
    for m in range(4):
        for c in range(ST):
            at = (m, slice(None), slice((c % 2) * TILE, (c % 2 + 1) * TILE))
            value = jnp.where(half == c // 2, own_ref[at].astype(F32), peer_ref[at].astype(F32))
            if m > 0:
                value = value * mask_ref[(front * UT + (m - 1) * 4 + group) * ST + c].astype(F32)
            out_ref[m, :, c * TILE : (c + 1) * TILE] = value.astype(BF16)


def initial(level, tile_mask, own, peer):
    vmem = pl.BlockSpec(memory_space=pltpu.VMEM)
    return pl.pallas_call(
        functools.partial(initial_kernel, level),
        out_shape=jax.ShapeDtypeStruct((4, TILE, S), BF16),
        in_specs=[pl.BlockSpec(memory_space=pltpu.SMEM), vmem, vmem],
        name=f"initial_{level}",
    )(tile_mask, own, peer)


def meet(devices):
    barrier = pltpu.get_barrier_semaphore()
    for device in devices:
        pl.semaphore_signal(
            barrier, inc=1, device_id=device, device_id_type=pl.DeviceIdType.MESH
        )
    pl.semaphore_wait(barrier, len(devices))


def neighbours():
    _, me = place()
    return [{"front": lax.rem(me + 1, RING)}, {"front": lax.rem(me + 3, RING)}]


class Ring:
    def __init__(self, view, size, sems, sibling, own):
        _, me = place()
        self.own = own
        self.view, self.size, self.sems, self.sibling = view, size, sems, sibling
        self.me = me
        self.right, self.left = lax.rem(me + 1, RING), lax.rem(me + 3, RING)
        self.across = lax.rem(me + 2, RING)

    def copy(self, k, c):
        part = self.size // 2
        to_right, to_left = {"front": self.right}, {"front": self.left}
        source, offset, rows, device = (
            (self.me, 0, part, to_right),
            (self.me, part, part, to_left),
            (self.me, part, part, to_right),
            (self.me, 0, part, to_left),
            (self.left, 0, part, to_right),
            (self.right, part, part, to_left),
            (self.me, 0, self.size, self.sibling),
            (self.left, 0, self.size, self.sibling),
            (self.right, 0, self.size, self.sibling),
            (self.across, 0, self.size, self.sibling),
        )[k]
        ref = self.view(source, offset, rows, c)
        return pltpu.make_async_remote_copy(
            src_ref=ref,
            dst_ref=ref,
            send_sem=self.sems.at[0, c, k],
            recv_sem=self.sems.at[1, c, k],
            device_id=device,
            device_id_type=pl.DeviceIdType.MESH,
        )

    def begin(self, c):
        for k in range(4):
            self.copy(k, c).start()
        if self.own:
            self.copy(6, c).start()

    def forward(self, c):
        self.copy(0, c).wait_recv()
        self.copy(4, c).start()
        self.copy(1, c).wait_recv()
        self.copy(5, c).start()
        self.copy(2, c).wait_recv()
        if self.sibling is not None:
            self.copy(7, c).start()
        self.copy(3, c).wait_recv()
        if self.sibling is not None:
            self.copy(8, c).start()

    def finish(self, c):
        self.copy(4, c).wait_recv()
        self.copy(5, c).wait_recv()
        if self.sibling is not None:
            self.copy(9, c).start()

    def settle(self, c):
        for k in range(10 if self.sibling is not None else 6):
            if k == 6 and not self.own:
                continue
            if k >= 6:
                self.copy(k, c).wait_recv()
            self.copy(k, c).wait_send()


def front_kernel(level, near_ref, init_ref, factor_ref, *refs):
    if level == 1:
        panels_ref, *refs = refs
    else:
        panel_ref, panels_ref, *refs = refs
    (a_ref, high_ref, low_ref, inv_ref, near_top, init_top, far_top, near_rest, init_rest, far_rest,
     local_sems, top_sems, rest_sems, pivot_sems, panel_sems) = refs
    leaf, me = place()
    core = lax.rem(leaf, 2)
    sibling = {"leaf": leaf + 1 - 2 * core}
    bit = lax.rem(leaf // level, 2)
    partner = {"leaf": leaf + level * (1 - 2 * bit)}
    half = TILE // 2
    low = pl.multiple_of(core * half, half)
    mine = pl.ds(low, half)
    theirs = mine if level == 2 else pl.ds(pl.multiple_of(half - low, half), half)
    quarter = lax.rem(leaf, 4)

    def tile(c):
        return pl.ds(pl.multiple_of(c * TILE, TILE), TILE)

    loads = [
        pltpu.make_async_copy(near_ref.at[0], near_top, local_sems.at[0]),
        pltpu.make_async_copy(init_ref.at[0, mine], init_top, local_sems.at[1]),
        pltpu.make_async_copy(near_ref.at[pl.ds(1, 3)], near_rest, local_sems.at[2]),
        pltpu.make_async_copy(init_ref.at[pl.ds(1, 3)], init_rest, local_sems.at[3]),
    ]
    for load in loads:
        load.start()
    meet(neighbours() + [sibling] + ([partner] if level == 2 else []))

    def top_copy(c):
        return pltpu.make_async_remote_copy(
            src_ref=near_top.at[theirs, tile(c)],
            dst_ref=far_top.at[:, tile(c)],
            send_sem=top_sems.at[0, c],
            recv_sem=top_sems.at[1, c],
            device_id=partner,
            device_id_type=pl.DeviceIdType.MESH,
        )

    def rest_copy(c, k):
        if level == 1:
            source, target = near_rest.at[:, :, tile(c)], far_rest.at[:, :, tile(c)]
        elif k == 0:
            source, target = near_rest.at[:, mine, tile(c)], far_rest.at[:, mine, tile(c)]
        else:
            source = target = far_rest.at[:, mine, tile(c)]
        return pltpu.make_async_remote_copy(
            src_ref=source,
            dst_ref=target,
            send_sem=rest_sems.at[0, c, k],
            recv_sem=rest_sems.at[1, c, k],
            device_id=partner if k == 0 else sibling,
            device_id_type=pl.DeviceIdType.MESH,
        )

    def rest_onward(c):
        if level == 2:
            rest_copy(c, 0).wait_recv()
            rest_copy(c, 1).start()

    pivots = Ring(
        lambda source, offset, rows, c: a_ref.at[
            pl.ds(pl.multiple_of(source * TILE + low + offset, half // 2), rows), tile(c)
        ],
        half,
        pivot_sems,
        sibling,
        True,
    )
    share = C // 2 if level == 1 else TILE
    base = core * share if level == 1 else 0
    panels = Ring(
        lambda source, offset, rows, c: panels_ref.at[
            source, pl.ds(pl.multiple_of(base + offset, share // 2), rows), tile(c)
        ],
        share,
        panel_sems,
        sibling if level == 1 else None,
        False,
    )

    loads[0].wait()
    for c in range(ST):
        top_copy(c).start()
    loads[1].wait()
    own_rows = pl.ds(pl.multiple_of(me * TILE + low, half), half)
    for c in range(ST):
        top_copy(c).wait_recv()
        there = slice(c * TILE, (c + 1) * TILE)
        a_ref[own_rows, there] = (
            near_top[mine, there].astype(F32)
            + far_top[:, there].astype(F32)
            + init_top[:, there].astype(F32)
        )
        pivots.begin(c)
    loads[2].wait()
    loads[3].wait()
    for c in range(ST):
        rest_copy(c, 0).start()
    pivots.forward(0)
    rest_onward(0)
    pivots.finish(0)

    def arrive(c):
        pivots.settle(c)
        rest_copy(c, 0).wait_send()
        if level == 2:
            rest_copy(c, 1).wait()
        else:
            rest_copy(c, 0).wait_recv()
        for m in range(3):
            rows = slice(S + m * TILE, S + (m + 1) * TILE)
            a_ref[rows, tile(c)] = (
                near_rest[m, :, tile(c)].astype(F32)
                + far_rest[m, :, tile(c)].astype(F32)
                + init_rest[m, :, tile(c)].astype(F32)
            )

    def left(rows, cols):
        return jnp.concatenate(
            [high_ref[rows, cols], low_ref[rows, cols], high_ref[rows, cols]], axis=1
        )

    def right(rows, cols):
        return jnp.concatenate(
            [high_ref[rows, cols], high_ref[rows, cols], low_ref[rows, cols]], axis=1
        )

    def step(g, _):
        c = g // 2
        even = g % 2 == 0
        odd = g % 2 == 1

        @pl.when(even)
        def _():
            arrive(c)

        for k in range(1, ST):

            @pl.when(g == 2 * k)
            def _():
                rows, done = slice(k * TILE, None), slice(0, k * TILE)
                there = slice(k * TILE, (k + 1) * TILE)
                a_ref[rows, there] -= (
                    dot_nt(high_ref[rows, done], high_ref[there, done])
                    + dot_nt(low_ref[rows, done], high_ref[there, done])
                    + dot_nt(high_ref[rows, done], low_ref[there, done])
                )

        cols = pl.ds(pl.multiple_of(g * G, G), G)
        invert_diagonal(a_ref.at[cols, cols], inv_ref)

        @pl.when(jnp.logical_and(even, g < 6))
        def _():
            pivots.forward(c + 1)
            rest_onward(c + 1)

        @pl.when(jnp.logical_and(odd, g < 6))
        def _():
            pivots.finish(c + 1)

        @pl.when(jnp.logical_and(even, g > 1))
        def _():
            panels.forward(c - 1)

        @pl.when(jnp.logical_and(odd, g > 1))
        def _():
            panels.finish(c - 1)

        inverse = right_parts(inv_ref[...])

        def panel(first, last):
            x = dot_nt(left_parts(a_ref[first:last, cols]), inverse)
            a_ref[first:last, cols] = x
            high, rest = split(x)
            high_ref[first:last, cols] = high
            low_ref[first:last, cols] = rest

        @pl.when(g < 4)
        def _():
            panel(0, S // 2)

        panel(S // 2, S + C)

        @pl.when(even)
        def _():
            after = pl.ds(pl.multiple_of(g * G + G, G), G)
            y = right(after, cols)

            def inside(first, last):
                a_ref[first:last, after] -= dot_nt(left(slice(first, last), cols), y)

            @pl.when(g < 4)
            def _():
                inside(0, S // 2)

            inside(S // 2, S + C)

        @pl.when(odd)
        def _():
            if level == 1:
                panels_ref[me, :, tile(c)] = high_ref[S:, tile(c)]
            else:
                panel_ref[:, tile(c)] = high_ref[S:, tile(c)]
                column = lax.rem(me + quarter, RING)
                part = lax.min((3 * quarter + column) // 4, 2)
                rows = pl.ds(pl.multiple_of(S + part * TILE, TILE), TILE)
                panels_ref[me, :, tile(c)] = high_ref[rows, tile(c)]
            panels.begin(c)

        return 0

    lax.fori_loop(0, S // G, step, 0)
    panels.forward(ST - 1)
    width = S // (2 * level)
    start = lax.rem(leaf, 2 * level) * width
    part = pl.ds(pl.multiple_of(start, width), width)
    row = lax.broadcasted_iota(jnp.int32, (TILE, width), 0) + me * TILE
    col = lax.broadcasted_iota(jnp.int32, (TILE, width), 1) + start
    factor_ref[0] = jnp.where(row >= col, a_ref[tile(me), part], 0.0)
    for m in range(1, 4):
        factor_ref[m] = a_ref[S + (m - 1) * TILE : S + m * TILE, part]
    panels.finish(ST - 1)
    for c in range(ST):
        panels.settle(c)
        top_copy(c).wait_send()


def front(level, near, init):
    hbm = pl.BlockSpec(memory_space=pl.ANY)
    vmem = pl.BlockSpec(memory_space=pltpu.VMEM)
    width = S // (2 * level)
    half = TILE // 2
    factor = jax.ShapeDtypeStruct((4, TILE, width), F32)
    if level == 1:
        outs = [factor, jax.ShapeDtypeStruct((RING, C, S), BF16)]
    else:
        outs = [
            factor,
            jax.ShapeDtypeStruct((C, S), BF16),
            jax.ShapeDtypeStruct((RING, TILE, S), BF16),
        ]
    return pl.pallas_call(
        functools.partial(front_kernel, level),
        out_shape=outs,
        in_specs=[hbm, hbm],
        out_specs=[vmem] * len(outs),
        scratch_shapes=[
            pltpu.VMEM((S + C, S), F32),
            pltpu.VMEM((S + C, S), BF16),
            pltpu.VMEM((S + C, S), BF16),
            pltpu.VMEM((G, G), F32),
            pltpu.VMEM((TILE, S), BF16),
            pltpu.VMEM((half, S), BF16),
            pltpu.VMEM((half, S), BF16),
            pltpu.VMEM((3, TILE, S), BF16),
            pltpu.VMEM((3, TILE, S), BF16),
            pltpu.VMEM((3, TILE, S), BF16),
            pltpu.SemaphoreType.DMA((4,)),
            pltpu.SemaphoreType.DMA((2, ST)),
            pltpu.SemaphoreType.DMA((2, ST, 2)),
            pltpu.SemaphoreType.DMA((2, ST, 10)),
            pltpu.SemaphoreType.DMA((2, ST, 10)),
        ],
        compiler_params=pltpu.CompilerParams(
            collective_id=level, has_side_effects=True, vmem_limit_bytes=VMEM_LIMIT
        ),
        cost_estimate=pl.CostEstimate(
            flops=50_000_000_000, bytes_accessed=20_000_000, transcendentals=0
        ),
        name=f"front_{level}",
    )(near, init)


def update_one_rows(map_one, map_two, panels, own, peer):
    here = jnp.stack(place()).astype(jnp.int32)

    def column(i, here_ref, two_ref):
        quarter = here_ref[0] % 4
        across = (quarter + 2) % 4
        t = jnp.where(i < 4, i, jnp.where(i < 7, 3 * quarter + i, 3 * across + i - 3))
        tile, live = source_of(two_ref, (here_ref[0] // 2) * UT, t % 4, t // 4)
        return t % 4, tile, live

    def panel_block(i, here_ref, one_ref, two_ref):
        other, tile, _ = column(i, here_ref, two_ref)
        return (other, tile, 0)

    def tile_block(s, side, i, here_ref, one_ref, two_ref):
        other, tile, _ = column(i, here_ref, two_ref)
        base = (here_ref[0] ^ side) * UT
        row, _ = source_of(one_ref, base, here_ref[1], 1 + s)
        col, _ = source_of(one_ref, base, other, 1 + tile)
        return (row, 0, col * 4 + other)

    def kernel(here_ref, one_ref, two_ref, x_ref, y_ref, *refs):
        tiles, pivot_out, near_out, far_out, total_ref = refs[:6], *refs[6:]
        i = pl.program_id(0)
        other, tile, col_live = column(i, here_ref, two_ref)
        product = dot_nt(x_ref[0], y_ref[0])
        for s in range(3):
            total = -product[s * TILE : (s + 1) * TILE, :]
            for side in (0, 1):
                base = (here_ref[0] ^ side) * UT
                _, live_row = source_of(one_ref, base, here_ref[1], 1 + s)
                _, live_col = source_of(one_ref, base, other, 1 + tile)
                live = jnp.logical_and(live_row, live_col)
                total = total + jnp.where(live, tiles[2 * s + side][0].astype(F32), 0.0)
            total_ref[s] = total.astype(BF16)

        def target(m):
            row, row_live = source_of(two_ref, (here_ref[0] // 2) * UT, here_ref[1], m)
            live = jnp.logical_and(row_live, col_live)
            return jnp.where(live, total_ref[row].astype(F32), 0.0).astype(BF16)

        @pl.when(i < 4)
        def _():
            for m in range(4):
                pivot_out[m] = target(m)

        @pl.when(jnp.logical_and(i >= 4, i < 7))
        def _():
            for m in range(1, 4):
                near_out[m - 1] = target(m)

        @pl.when(i >= 7)
        def _():
            for m in range(1, 4):
                far_out[m - 1] = target(m)

    return pl.pallas_call(
        kernel,
        out_shape=[
            jax.ShapeDtypeStruct((4, TILE, S), BF16),
            jax.ShapeDtypeStruct((3, TILE, C), BF16),
            jax.ShapeDtypeStruct((3, TILE, C), BF16),
        ],
        grid_spec=pltpu.PrefetchScalarGridSpec(
            num_scalar_prefetch=3,
            grid=(10,),
            in_specs=[
                pl.BlockSpec((1, C, S), lambda i, here_ref, *_: (here_ref[1], 0, 0)),
                pl.BlockSpec((1, TILE, S), panel_block),
                *[
                    pl.BlockSpec((1, TILE, TILE), functools.partial(tile_block, s, side))
                    for s in range(3)
                    for side in (0, 1)
                ],
            ],
            out_specs=[
                pl.BlockSpec((4, TILE, TILE), lambda i, *_: (0, 0, jnp.minimum(i, 3))),
                pl.BlockSpec((3, TILE, TILE), lambda i, *_: (0, 0, jnp.clip(i - 4, 0, 2))),
                pl.BlockSpec((3, TILE, TILE), lambda i, *_: (0, 0, jnp.clip(i - 7, 0, 2))),
            ],
            scratch_shapes=[pltpu.VMEM((3, TILE, TILE), BF16)],
        ),
        compiler_params=pltpu.CompilerParams(vmem_limit_bytes=VMEM_LIMIT),
        name="update_1",
    )(here, map_one, map_two, panels, panels, *([own, peer] * 3))


def update_two_kernel(x_ref, y_ref, near_ref, far_ref, out_ref):
    leaf, _ = place()
    quarter = lax.rem(leaf, 4)
    for i in range(3):
        there = slice(i * TILE, (i + 1) * TILE)
        product = dot_nt(x_ref[...], y_ref[lax.rem(3 * quarter + i, RING)])
        for m in range(3):
            front = near_ref[m, :, there].astype(F32) + far_ref[m, :, there].astype(F32)
            out_ref[m, :, there] = (front - product[m * TILE : (m + 1) * TILE, :]).astype(BF16)


def update_two_rows(panel, panels, near, far):
    vmem = pl.BlockSpec(memory_space=pltpu.VMEM)
    return pl.pallas_call(
        update_two_kernel,
        out_shape=jax.ShapeDtypeStruct((3, TILE, C), BF16),
        in_specs=[vmem] * 4,
        compiler_params=pltpu.CompilerParams(vmem_limit_bytes=VMEM_LIMIT),
        name="update_2",
    )(panel, panels, near, far)


def join_halves(mine, other, position):
    lower_first = jnp.concatenate([mine, other], axis=-1)
    upper_first = jnp.concatenate([other, mine], axis=-1)
    return jnp.where(position == 0, lower_first, upper_first)


def body(child_update, sep_one, sep_two, map_one, map_two, mask_one, mask_two):
    leaf = lax.axis_index("leaf")
    own = child_update[0, 0, 0]
    entries = sep_one[0, 0, 0]
    quarter = sep_two[0, 0, 0]
    map_one, map_two = map_one.reshape(-1), map_two.reshape(-1)
    entries_peer, quarter_peer, peer = swapped((entries, quarter, own), "leaf", 0)
    near = spread(map_one, own)
    init = initial(1, mask_one.reshape(-1), entries, entries_peer)
    half = join_halves(quarter, quarter_peer, leaf % 2)
    half_far = swapped(half, "leaf", 1)
    factor_one, panels = front(1, near, init)
    panels, half, half_far = lax.optimization_barrier((panels, half, half_far))
    init_two = initial(2, mask_two.reshape(-1), half, half_far)
    near, rest_near, rest_far = update_one_rows(map_one, map_two, panels, own, peer)
    rest_far = swapped(rest_far, "leaf", 1)
    factor_two, panel, panels = front(2, near, init_two)
    panel, rest_far = lax.optimization_barrier((panel, rest_far))
    update_two = update_two_rows(panel, panels, rest_near, rest_far)
    return (factor_one[None, None, None], factor_two[None, None, None], update_two[None, None, None])


def solution(mesh):
    split_spec = P("leaf", "front", None, None, None, None)
    return jax.shard_map(
        body,
        mesh=mesh,
        in_specs=(split_spec, split_spec, split_spec, P(), P(), P(), P()),
        out_specs=(split_spec, split_spec, split_spec),
        check_vma=False,
    )
```

```python
import functools

import jax
import jax.numpy as jnp
from jax import lax
from jax.experimental import pallas as pl
from jax.experimental.pallas import tpu as pltpu
from jax.sharding import PartitionSpec as P

TILE = 256
ST = 4
UT = 12
RING = 4
S = 1024
U = 3072
C = 768
G = 128
F32 = jnp.float32
BF16 = jnp.bfloat16
VMEM_LIMIT = 60 * 1024 * 1024


def swapped(value, axis, apart):
    mask = 2**apart
    pairs = [(source, source ^ mask) for source in range(lax.axis_size(axis))]
    return lax.ppermute(value, axis, pairs)


def dot_nt(x, y):
    return lax.dot_general(x, y, (((1,), (1,)), ((), ())), preferred_element_type=F32)


def split(x):
    high = x.astype(BF16)
    return high, (x - high.astype(F32)).astype(BF16)


def left_parts(x):
    high, low = split(x)
    return jnp.concatenate([high, low, high], axis=1)


def right_parts(x):
    high, low = split(x)
    return jnp.concatenate([high, high, low], axis=1)


def source_of(map_ref, child, group, slot):
    first = map_ref[child, 0, group, 0] == slot
    second = map_ref[child, 0, group, 1] == slot
    third = map_ref[child, 0, group, 2] == slot
    index = jnp.where(first, 0, jnp.where(second, 1, 2))
    live = jnp.logical_or(first, jnp.logical_or(second, third))
    return index, live


def invert_diagonal(block_ref, inverse_ref):
    sub = lax.broadcasted_iota(jnp.int32, (8, G), 0)
    lane = lax.broadcasted_iota(jnp.int32, (8, G), 1)
    slabs = G // 8
    rest = [block_ref[8 * r : 8 * r + 8, :] for r in range(slabs)]
    unit = [jnp.where(lane == sub + 8 * r, 1.0, 0.0).astype(F32) for r in range(slabs)]

    def lanes(v, c):
        return jnp.broadcast_to(v[:, c : c + 1], (8, G))

    def rows(v, i):
        return jnp.broadcast_to(v[i : i + 1, :], (8, G))

    for t in range(slabs):
        k = 8 * t
        cols = [lanes(rest[t], k + i) for i in range(8)]
        a = {(i, j): rows(cols[j], i) for j in range(8) for i in range(j, 8)}
        low = {}
        scale = []
        for i in range(8):
            scale.append(lax.rsqrt(a[i, i]))
            for j in range(i + 1, 8):
                low[j, i] = a[j, i] * scale[i]
            for j in range(i + 1, 8):
                for m in range(j, 8):
                    a[m, j] = a[m, j] - low[m, i] * low[j, i]

        def forward(pick):
            out = []
            for i in range(8):
                x = pick(i)
                for j in range(i):
                    x = x - low[i, j] * out[j]
                out.append(x * scale[i])
            return out

        upper = forward(lambda i: rows(rest[t], i))
        inv = forward(lambda i: rows(unit[t], i))
        packed = inv[0]
        for i in range(1, 8):
            packed = jnp.where(sub == i, inv[i], packed)
        inverse_ref[k : k + 8, :] = packed
        for r in range(t + 1, slabs):
            column = []
            for i in range(8):
                x = lanes(rest[r], k + i)
                for j in range(i):
                    x = x - column[j] * low[i, j]
                column.append(x * scale[i])
            for i in range(8):
                rest[r] = rest[r] - column[i] * upper[i]
                unit[r] = unit[r] - column[i] * inv[i]


def place():
    return lax.axis_index("leaf"), lax.axis_index("front")


def spread_kernel(map_ref, child_ref, out_ref, sems):
    leaf, group = place()
    copies = []
    for m in range(4):
        row, row_live = source_of(map_ref, leaf, group, m)
        for c in range(ST):
            col, col_live = source_of(map_ref, leaf, c, 0)
            start = pl.multiple_of((col * 4 + c) * TILE, TILE)
            there = slice(c * TILE, (c + 1) * TILE)
            copy = pltpu.make_async_copy(
                child_ref.at[row, :, pl.ds(start, TILE)], out_ref.at[m, :, there], sems.at[m, c]
            )
            copy.start()
            copies.append((copy, m, there, jnp.logical_and(row_live, col_live)))
    for copy, m, there, live in copies:
        copy.wait()

        @pl.when(jnp.logical_not(live))
        def _():
            out_ref[m, :, there] = jnp.zeros((TILE, TILE), BF16)


def spread(tile_map, child):
    return pl.pallas_call(
        spread_kernel,
        out_shape=jax.ShapeDtypeStruct((4, TILE, S), BF16),
        in_specs=[pl.BlockSpec(memory_space=pltpu.SMEM), pl.BlockSpec(memory_space=pl.ANY)],
        scratch_shapes=[pltpu.SemaphoreType.DMA((4, ST))],
        name="spread",
    )(tile_map, child)


def meet(devices):
    barrier = pltpu.get_barrier_semaphore()
    for device in devices:
        pl.semaphore_signal(
            barrier, inc=1, device_id=device, device_id_type=pl.DeviceIdType.MESH
        )
    pl.semaphore_wait(barrier, len(devices))


def neighbours():
    _, me = place()
    return [{"front": lax.rem(me + 1, RING)}, {"front": lax.rem(me + 3, RING)}]


class Ring:
    def __init__(self, view, size, sems, sibling, own, lower):
        _, me = place()
        self.own, self.lower = own, lower
        self.view, self.size, self.sems, self.sibling = view, size, sems, sibling
        self.me = me
        self.right, self.left = lax.rem(me + 1, RING), lax.rem(me + 3, RING)
        self.across = lax.rem(me + 2, RING)

    def copy(self, k, c):
        part = self.size // 2
        to_right, to_left = {"front": self.right}, {"front": self.left}
        source, offset, rows, device = (
            (self.me, 0, part, to_right),
            (self.me, part, part, to_left),
            (self.me, part, part, to_right),
            (self.me, 0, part, to_left),
            (self.left, 0, part, to_right),
            (self.right, part, part, to_left),
            (self.me, 0, self.size, self.sibling),
            (self.left, 0, self.size, self.sibling),
            (self.right, 0, self.size, self.sibling),
            (self.across, 0, self.size, self.sibling),
        )[k]
        ref = self.view(source, offset, rows, c)
        return pltpu.make_async_remote_copy(
            src_ref=ref,
            dst_ref=ref,
            send_sem=self.sems.at[0, c, k],
            recv_sem=self.sems.at[1, c, k],
            device_id=device,
            device_id_type=pl.DeviceIdType.MESH,
        )

    def sent(self, k):
        return (
            self.me, self.me, self.me, self.me, self.left, self.right,
            self.me, self.left, self.right, self.across,
        )[k]

    def received(self, k):
        return (
            self.left, self.right, self.left, self.right, self.across, self.across,
            self.me, self.left, self.right, self.across,
        )[k]

    def act(self, source, c, action):
        if self.lower:
            pl.when(source >= c)(action)
        else:
            action()

    def start(self, k, c):
        self.act(self.sent(k), c, lambda: self.copy(k, c).start())

    def wait_recv(self, k, c):
        self.act(self.received(k), c, lambda: self.copy(k, c).wait_recv())

    def wait_send(self, k, c):
        self.act(self.sent(k), c, lambda: self.copy(k, c).wait_send())

    def begin(self, c):
        for k in range(4):
            self.start(k, c)
        if self.own:
            self.start(6, c)

    def forward(self, c):
        for k in range(4):
            self.wait_recv(k, c)
            if k < 2:
                self.start(4 + k, c)
            elif self.sibling is not None:
                self.start(5 + k, c)

    def finish(self, c):
        self.wait_recv(4, c)
        self.wait_recv(5, c)
        if self.sibling is not None:
            self.start(9, c)

    def settle(self, c):
        for k in range(10 if self.sibling is not None else 6):
            if k == 6 and not self.own:
                continue
            if k >= 6:
                self.wait_recv(k, c)
            self.wait_send(k, c)


def front_kernel(level, mask_ref, near_ref, own_ref, peer_ref, *refs):
    if level == 1:
        factor_ref, panels_ref, *refs = refs
    else:
        given_ref, factor_ref, panel_ref, panels_ref, taken_ref, given_buf, given_sems, *refs = refs
    (a_ref, high_ref, low_ref, inv_ref, near_top, init_top, far_top, near_rest, init_rest, far_rest,
     local_sems, top_sems, rest_sems, pivot_sems, panel_sems) = refs
    leaf, me = place()
    core = lax.rem(leaf, 2)
    sibling = {"leaf": leaf + 1 - 2 * core}
    bit = lax.rem(leaf // level, 2)
    partner = {"leaf": leaf + level * (1 - 2 * bit)}
    half = TILE // 2
    low = pl.multiple_of(core * half, half)
    mine = pl.ds(low, half)
    theirs = mine if level == 2 else pl.ds(pl.multiple_of(half - low, half), half)
    quarter = lax.rem(leaf, 4)

    def tile(c):
        return pl.ds(pl.multiple_of(c * TILE, TILE), TILE)

    loads = [
        pltpu.make_async_copy(near_ref.at[0], near_top, local_sems.at[0]),
        pltpu.make_async_copy(own_ref.at[0, mine], init_top.at[bit], local_sems.at[1]),
        pltpu.make_async_copy(peer_ref.at[0, mine], init_top.at[1 - bit], local_sems.at[2]),
        pltpu.make_async_copy(near_ref.at[pl.ds(1, 3)], near_rest, local_sems.at[3]),
        pltpu.make_async_copy(own_ref.at[pl.ds(1, 3)], init_rest.at[bit], local_sems.at[4]),
        pltpu.make_async_copy(peer_ref.at[pl.ds(1, 3)], init_rest.at[1 - bit], local_sems.at[5]),
    ]
    if level == 2:
        loads.append(pltpu.make_async_copy(given_ref, given_buf, local_sems.at[6]))
    for load in loads:
        load.start()
    meet(neighbours() + [sibling] + ([partner] if level == 2 else []))

    def top_copy(c):
        return pltpu.make_async_remote_copy(
            src_ref=near_top.at[theirs, tile(c)],
            dst_ref=far_top.at[:, tile(c)],
            send_sem=top_sems.at[0, c],
            recv_sem=top_sems.at[1, c],
            device_id=partner,
            device_id_type=pl.DeviceIdType.MESH,
        )

    def rest_copy(c, k):
        if level == 1:
            source, target = near_rest.at[:, :, tile(c)], far_rest.at[:, :, tile(c)]
        elif k == 0:
            source, target = near_rest.at[:, mine, tile(c)], far_rest.at[:, mine, tile(c)]
        else:
            source = target = far_rest.at[:, mine, tile(c)]
        return pltpu.make_async_remote_copy(
            src_ref=source,
            dst_ref=target,
            send_sem=rest_sems.at[0, c, k],
            recv_sem=rest_sems.at[1, c, k],
            device_id=partner if k == 0 else sibling,
            device_id_type=pl.DeviceIdType.MESH,
        )

    def rest_onward(c):
        if level == 2:
            rest_copy(c, 0).wait_recv()
            rest_copy(c, 1).start()

    pivots = Ring(
        lambda source, offset, rows, c: a_ref.at[
            pl.ds(pl.multiple_of(source * TILE + low + offset, half // 2), rows), tile(c)
        ],
        half,
        pivot_sems,
        sibling,
        True,
        True,
    )
    share = C // 2 if level == 1 else TILE
    base = core * share if level == 1 else 0
    panels = Ring(
        lambda source, offset, rows, c: panels_ref.at[
            source, pl.ds(pl.multiple_of(base + offset, share // 2), rows), tile(c)
        ],
        share,
        panel_sems,
        sibling if level == 1 else None,
        False,
        False,
    )

    def give():
        return pltpu.make_async_remote_copy(
            src_ref=given_buf,
            dst_ref=taken_ref,
            send_sem=given_sems.at[0],
            recv_sem=given_sems.at[1],
            device_id=partner,
            device_id_type=pl.DeviceIdType.MESH,
        )

    loads[0].wait()
    for c in range(ST):
        top_copy(c).start()
    loads[1].wait()
    loads[2].wait()
    own_rows = pl.ds(pl.multiple_of(me * TILE + low, half), half)
    for c in range(ST):
        top_copy(c).wait_recv()
        there = slice(c * TILE, (c + 1) * TILE)
        a_ref[own_rows, there] = (
            near_top[mine, there].astype(F32)
            + far_top[:, there].astype(F32)
            + init_top[c // 2, :, (c % 2) * TILE : (c % 2 + 1) * TILE].astype(F32)
        )
        if c == 0:
            pivots.begin(0)
    for load in loads[3:]:
        load.wait()
    for c in range(ST):
        rest_copy(c, 0).start()
    pivots.forward(0)
    pivots.begin(1)
    rest_onward(0)
    pivots.finish(0)

    def arrive(c):
        pivots.settle(c)
        rest_copy(c, 0).wait_send()
        if level == 2:
            rest_copy(c, 1).wait()
        else:
            rest_copy(c, 0).wait_recv()
        for m in range(3):
            rows = slice(S + m * TILE, S + (m + 1) * TILE)
            keep = mask_ref[leaf // (2 * level), 0, 4 * m + me, c].astype(F32)
            a_ref[rows, tile(c)] = (
                near_rest[m, :, tile(c)].astype(F32)
                + far_rest[m, :, tile(c)].astype(F32)
                + init_rest[c // 2, m, :, tile(c % 2)].astype(F32) * keep
            )

    def left(rows, cols):
        return jnp.concatenate(
            [high_ref[rows, cols], low_ref[rows, cols], high_ref[rows, cols]], axis=1
        )

    def right(rows, cols):
        return jnp.concatenate(
            [high_ref[rows, cols], high_ref[rows, cols], low_ref[rows, cols]], axis=1
        )

    def step(g, _):
        c = g // 2
        even = g % 2 == 0
        odd = g % 2 == 1

        @pl.when(even)
        def _():
            arrive(c)

        for k in range(1, ST):

            @pl.when(g == 2 * k)
            def _():
                rows, done = slice(k * TILE, None), slice(0, k * TILE)
                there = slice(k * TILE, (k + 1) * TILE)
                a_ref[rows, there] -= (
                    dot_nt(high_ref[rows, done], high_ref[there, done])
                    + dot_nt(low_ref[rows, done], high_ref[there, done])
                    + dot_nt(high_ref[rows, done], low_ref[there, done])
                )

        cols = pl.ds(pl.multiple_of(g * G, G), G)
        invert_diagonal(a_ref.at[cols, cols], inv_ref)

        @pl.when(jnp.logical_and(even, g < 6))
        def _():
            pivots.forward(c + 1)
            rest_onward(c + 1)

        @pl.when(jnp.logical_and(even, g < 4))
        def _():
            pivots.begin(c + 2)

        if level == 2:

            @pl.when(g == 4)
            def _():
                give().start()

        @pl.when(jnp.logical_and(odd, g < 6))
        def _():
            pivots.finish(c + 1)

        inverse = right_parts(inv_ref[...])

        def panel(first, last):
            x = dot_nt(left_parts(a_ref[first:last, cols]), inverse)
            a_ref[first:last, cols] = x
            high, rest = split(x)
            high_ref[first:last, cols] = high
            low_ref[first:last, cols] = rest

        @pl.when(g < 4)
        def _():
            panel(0, S // 2)

        panel(S // 2, S + C)

        @pl.when(even)
        def _():
            after = pl.ds(pl.multiple_of(g * G + G, G), G)
            y = right(after, cols)

            def inside(first, last):
                a_ref[first:last, after] -= dot_nt(left(slice(first, last), cols), y)

            @pl.when(g < 4)
            def _():
                inside(0, S // 2)

            inside(S // 2, S + C)

        @pl.when(jnp.logical_and(even, g > 1))
        def _():
            panels.forward(c - 1)

        @pl.when(jnp.logical_and(odd, g > 1))
        def _():
            panels.finish(c - 1)

        @pl.when(odd)
        def _():
            if level == 1:
                panels_ref[me, :, tile(c)] = high_ref[S:, tile(c)]
            else:
                panel_ref[:, tile(c)] = high_ref[S:, tile(c)]
                column = lax.rem(me + quarter, RING)
                part = lax.min((3 * quarter + column) // 4, 2)
                rows = pl.ds(pl.multiple_of(S + part * TILE, TILE), TILE)
                panels_ref[me, :, tile(c)] = high_ref[rows, tile(c)]
            panels.begin(c)

        return 0

    lax.fori_loop(0, S // G, step, 0)
    panels.forward(ST - 1)
    width = S // (2 * level)
    start = lax.rem(leaf, 2 * level) * width
    part = pl.ds(pl.multiple_of(start, width), width)
    row = lax.broadcasted_iota(jnp.int32, (TILE, width), 0) + me * TILE
    col = lax.broadcasted_iota(jnp.int32, (TILE, width), 1) + start
    factor_ref[0] = jnp.where(row >= col, a_ref[tile(me), part], 0.0)
    for m in range(1, 4):
        factor_ref[m] = a_ref[S + (m - 1) * TILE : S + m * TILE, part]
    panels.finish(ST - 1)
    for c in range(ST):
        panels.settle(c)
        top_copy(c).wait_send()
    if level == 2:
        give().wait()


def front(level, tile_mask, near, own, peer, given=None):
    hbm = pl.BlockSpec(memory_space=pl.ANY)
    vmem = pl.BlockSpec(memory_space=pltpu.VMEM)
    width = S // (2 * level)
    half = TILE // 2
    factor = jax.ShapeDtypeStruct((4, TILE, width), F32)
    if level == 1:
        outs = [factor, jax.ShapeDtypeStruct((RING, C, S), BF16)]
    else:
        outs = [
            factor,
            jax.ShapeDtypeStruct((C, S), BF16),
            jax.ShapeDtypeStruct((RING, TILE, S), BF16),
            jax.ShapeDtypeStruct((3, TILE, C), BF16),
        ]
    given = [] if level == 1 else [given]
    return pl.pallas_call(
        functools.partial(front_kernel, level),
        out_shape=outs,
        in_specs=[pl.BlockSpec(memory_space=pltpu.SMEM)] + [hbm] * (3 + len(given)),
        out_specs=[vmem] * len(outs),
        scratch_shapes=[
            *([pltpu.VMEM((3, TILE, C), BF16), pltpu.SemaphoreType.DMA((2,))] if given else []),
            pltpu.VMEM((S + C, S), F32),
            pltpu.VMEM((S + C, S), BF16),
            pltpu.VMEM((S + C, S), BF16),
            pltpu.VMEM((G, G), F32),
            pltpu.VMEM((TILE, S), BF16),
            pltpu.VMEM((2, half, S // 2), BF16),
            pltpu.VMEM((half, S), BF16),
            pltpu.VMEM((3, TILE, S), BF16),
            pltpu.VMEM((2, 3, TILE, S // 2), BF16),
            pltpu.VMEM((3, TILE, S), BF16),
            pltpu.SemaphoreType.DMA((7,)),
            pltpu.SemaphoreType.DMA((2, ST)),
            pltpu.SemaphoreType.DMA((2, ST, 2)),
            pltpu.SemaphoreType.DMA((2, ST, 10)),
            pltpu.SemaphoreType.DMA((2, ST, 10)),
        ],
        compiler_params=pltpu.CompilerParams(
            collective_id=level, has_side_effects=True, vmem_limit_bytes=VMEM_LIMIT
        ),
        cost_estimate=pl.CostEstimate(
            flops=50_000_000_000, bytes_accessed=20_000_000, transcendentals=0
        ),
        name=f"front_{level}",
    )(tile_mask, near, own, peer, *given)


def update_one_kernel(one_ref, two_ref, panels_ref, own_ref, peer_ref, pivot_out, near_out, far_out,
                      x_buf, y_buf, tiles, total_ref, sems, x_sem):
    leaf, group = place()
    quarter = leaf % 4
    across = (quarter + 2) % 4
    sides = (own_ref, peer_ref)

    def column(i):
        t = jnp.where(i < 4, i, jnp.where(i < 7, 3 * quarter + i, 3 * across + i - 3))
        tile, live = source_of(two_ref, leaf // 2, t % 4, t // 4)
        return t % 4, tile, live

    def there(i):
        return pl.ds(pl.multiple_of(i * TILE, TILE), TILE)

    def copy(source, target, i, k):
        return pltpu.make_async_copy(source, target, sems.at[i, k])

    rows = [[source_of(one_ref, leaf ^ side, group, 1 + s) for s in range(3)] for side in (0, 1)]
    targets = [source_of(two_ref, leaf // 2, group, m) for m in range(4)]
    x_copy = pltpu.make_async_copy(panels_ref.at[group], x_buf, x_sem)
    x_copy.start()

    def start(i, _):
        other, tile, _ = column(i)
        copy(panels_ref.at[other, there(tile)], y_buf.at[i], i, 0).start()
        for side in (0, 1):
            col, _ = source_of(one_ref, leaf ^ side, other, 1 + tile)
            for s in range(3):
                copy(
                    sides[side].at[rows[side][s][0], :, there(col * 4 + other)],
                    tiles.at[side, s, :, there(i)],
                    i,
                    1 + 3 * side + s,
                ).start()
        return 0

    lax.fori_loop(0, 10, start, 0)
    x_copy.wait()

    def step(i, _):
        other, tile, col_live = column(i)
        copy(panels_ref.at[0, there(0)], y_buf.at[i], i, 0).wait()
        product = dot_nt(x_buf[...], y_buf[i])
        for s in range(3):
            total = -product[s * TILE : (s + 1) * TILE, :]
            for side in (0, 1):
                slot = tiles.at[side, s, :, there(i)]
                copy(own_ref.at[0, :, there(0)], slot, i, 1 + 3 * side + s).wait()
                _, live = source_of(one_ref, leaf ^ side, other, 1 + tile)
                live = jnp.logical_and(rows[side][s][1], live)
                total = total + jnp.where(live, slot[...].astype(F32), 0.0)
            total_ref[s] = total.astype(BF16)

        def target(m):
            live = jnp.logical_and(targets[m][1], col_live)
            return jnp.where(live, total_ref[targets[m][0]].astype(F32), 0.0).astype(BF16)

        @pl.when(i < 4)
        def _():
            for m in range(4):
                pivot_out[m, :, there(i)] = target(m)

        @pl.when(jnp.logical_and(i >= 4, i < 7))
        def _():
            for m in range(1, 4):
                near_out[m - 1, :, there(i - 4)] = target(m)

        @pl.when(i >= 7)
        def _():
            for m in range(1, 4):
                far_out[m - 1, :, there(i - 7)] = target(m)

        return 0

    lax.fori_loop(0, 10, step, 0)


def update_one_rows(map_one, map_two, panels, own, peer):
    smem = pl.BlockSpec(memory_space=pltpu.SMEM)
    hbm = pl.BlockSpec(memory_space=pl.ANY)
    return pl.pallas_call(
        update_one_kernel,
        out_shape=[
            jax.ShapeDtypeStruct((4, TILE, S), BF16),
            jax.ShapeDtypeStruct((3, TILE, C), BF16),
            jax.ShapeDtypeStruct((3, TILE, C), BF16),
        ],
        in_specs=[smem, smem, hbm, hbm, hbm],
        scratch_shapes=[
            pltpu.VMEM((C, S), BF16),
            pltpu.VMEM((10, TILE, S), BF16),
            pltpu.VMEM((2, 3, TILE, 10 * TILE), BF16),
            pltpu.VMEM((3, TILE, TILE), BF16),
            pltpu.SemaphoreType.DMA((10, 7)),
            pltpu.SemaphoreType.DMA,
        ],
        compiler_params=pltpu.CompilerParams(vmem_limit_bytes=VMEM_LIMIT),
        name="update_1",
    )(map_one, map_two, panels, own, peer)


def update_two_kernel(x_ref, y_ref, near_ref, far_ref, out_ref):
    leaf, _ = place()
    quarter = lax.rem(leaf, 4)
    for i in range(3):
        there = slice(i * TILE, (i + 1) * TILE)
        product = dot_nt(x_ref[...], y_ref[lax.rem(3 * quarter + i, RING)])
        for m in range(3):
            front = near_ref[m, :, there].astype(F32) + far_ref[m, :, there].astype(F32)
            out_ref[m, :, there] = (front - product[m * TILE : (m + 1) * TILE, :]).astype(BF16)


def update_two_rows(panel, panels, near, far):
    vmem = pl.BlockSpec(memory_space=pltpu.VMEM)
    return pl.pallas_call(
        update_two_kernel,
        out_shape=jax.ShapeDtypeStruct((3, TILE, C), BF16),
        in_specs=[vmem] * 4,
        compiler_params=pltpu.CompilerParams(vmem_limit_bytes=VMEM_LIMIT),
        name="update_2",
    )(panel, panels, near, far)


def join_halves(mine, other, position):
    lower_first = jnp.concatenate([mine, other], axis=-1)
    upper_first = jnp.concatenate([other, mine], axis=-1)
    return jnp.where(position == 0, lower_first, upper_first)


def body(child_update, sep_one, sep_two, map_one, map_two, mask_one, mask_two):
    leaf = lax.axis_index("leaf")
    own = child_update[0, 0, 0]
    entries = sep_one[0, 0, 0]
    quarter = sep_two[0, 0, 0]
    entries_peer, quarter_peer, peer = swapped((entries, quarter, own), "leaf", 0)
    near = spread(map_one, own)
    half = join_halves(quarter, quarter_peer, leaf % 2)
    half_far = swapped(half, "leaf", 1)
    factor_one, panels = front(1, mask_one, near, entries, entries_peer)
    panels, half, half_far = lax.optimization_barrier((panels, half, half_far))
    near, rest, given = update_one_rows(map_one, map_two, panels, own, peer)
    factor_two, panel, panels, taken = front(2, mask_two, near, half, half_far, given)
    update_two = update_two_rows(panel, panels, rest, taken)
    return (factor_one[None, None, None], factor_two[None, None, None], update_two[None, None, None])


def solution(mesh):
    split_spec = P("leaf", "front", None, None, None, None)
    return jax.shard_map(
        body,
        mesh=mesh,
        in_specs=(split_spec, split_spec, split_spec, P(), P(), P(), P()),
        out_specs=(split_spec, split_spec, split_spec),
        check_vma=False,
    )
```

```python
import functools

import jax
import jax.numpy as jnp
from jax import lax
from jax.experimental import pallas as pl
from jax.experimental.pallas import tpu as pltpu
from jax.sharding import PartitionSpec as P

TILE = 256
ST = 4
UT = 12
RING = 4
S = 1024
U = 3072
C = 768
G = 128
F32 = jnp.float32
BF16 = jnp.bfloat16
VMEM_LIMIT = 60 * 1024 * 1024


def swapped(value, axis, apart):
    mask = 2**apart
    pairs = [(source, source ^ mask) for source in range(lax.axis_size(axis))]
    return lax.ppermute(value, axis, pairs)


def dot_nt(x, y):
    return lax.dot_general(x, y, (((1,), (1,)), ((), ())), preferred_element_type=F32)


def split(x):
    high = x.astype(BF16)
    return high, (x - high.astype(F32)).astype(BF16)


def left_parts(x):
    high, low = split(x)
    return jnp.concatenate([high, low, high], axis=1)


def right_parts(x):
    high, low = split(x)
    return jnp.concatenate([high, high, low], axis=1)


def source_of(map_ref, child, group, slot):
    first = map_ref[0, group, child] == slot
    second = map_ref[1, group, child] == slot
    third = map_ref[2, group, child] == slot
    index = jnp.where(first, 0, jnp.where(second, 1, 2))
    live = jnp.logical_or(first, jnp.logical_or(second, third))
    return index, live


def invert_diagonal(block_ref, inverse_ref):
    sub = lax.broadcasted_iota(jnp.int32, (8, G), 0)
    lane = lax.broadcasted_iota(jnp.int32, (8, G), 1)
    slabs = G // 8
    rest = [block_ref[8 * r : 8 * r + 8, :] for r in range(slabs)]
    unit = [jnp.where(lane == sub + 8 * r, 1.0, 0.0).astype(F32) for r in range(slabs)]

    def lanes(v, c):
        return jnp.broadcast_to(v[:, c : c + 1], (8, G))

    def rows(v, i):
        return jnp.broadcast_to(v[i : i + 1, :], (8, G))

    for t in range(slabs):
        k = 8 * t
        cols = [lanes(rest[t], k + i) for i in range(8)]
        a = {(i, j): rows(cols[j], i) for j in range(8) for i in range(j, 8)}
        low = {}
        scale = []
        for i in range(8):
            scale.append(lax.rsqrt(a[i, i]))
            for j in range(i + 1, 8):
                low[j, i] = a[j, i] * scale[i]
            for j in range(i + 1, 8):
                for m in range(j, 8):
                    a[m, j] = a[m, j] - low[m, i] * low[j, i]

        def forward(pick):
            out = []
            for i in range(8):
                x = pick(i)
                for j in range(i):
                    x = x - low[i, j] * out[j]
                out.append(x * scale[i])
            return out

        upper = forward(lambda i: rows(rest[t], i))
        inv = forward(lambda i: rows(unit[t], i))
        packed = inv[0]
        for i in range(1, 8):
            packed = jnp.where(sub == i, inv[i], packed)
        inverse_ref[k : k + 8, :] = packed
        for r in range(t + 1, slabs):
            column = []
            for i in range(8):
                x = lanes(rest[r], k + i)
                for j in range(i):
                    x = x - column[j] * low[i, j]
                column.append(x * scale[i])
            for i in range(8):
                rest[r] = rest[r] - column[i] * upper[i]
                unit[r] = unit[r] - column[i] * inv[i]


def place():
    return lax.axis_index("leaf"), lax.axis_index("front")


def spread_kernel(maps_ref, child_ref, out_ref, map_ref, map_sem, sems):
    leaf, group = place()
    fetch = pltpu.make_async_copy(maps_ref, map_ref, map_sem)
    fetch.start()
    fetch.wait()
    copies = []
    for m in range(4):
        row, row_live = source_of(map_ref, leaf, group, m)
        for c in range(ST):
            col, col_live = source_of(map_ref, leaf, c, 0)
            start = pl.multiple_of((col * 4 + c) * TILE, TILE)
            there = slice(c * TILE, (c + 1) * TILE)
            copy = pltpu.make_async_copy(
                child_ref.at[row, :, pl.ds(start, TILE)], out_ref.at[m, :, there], sems.at[m, c]
            )
            copy.start()
            copies.append((copy, m, there, jnp.logical_and(row_live, col_live)))
    for copy, m, there, live in copies:
        copy.wait()

        @pl.when(jnp.logical_not(live))
        def _():
            out_ref[m, :, there] = jnp.zeros((TILE, TILE), BF16)


def spread(tile_map, child):
    return pl.pallas_call(
        spread_kernel,
        out_shape=jax.ShapeDtypeStruct((4, TILE, S), BF16),
        in_specs=[pl.BlockSpec(memory_space=pl.ANY)] * 2,
        scratch_shapes=[
            pltpu.SMEM(tile_map.shape, jnp.int32),
            pltpu.SemaphoreType.DMA,
            pltpu.SemaphoreType.DMA((4, ST)),
        ],
        name="spread",
    )(tile_map, child)


def meet(devices):
    barrier = pltpu.get_barrier_semaphore()
    for device in devices:
        pl.semaphore_signal(
            barrier, inc=1, device_id=device, device_id_type=pl.DeviceIdType.MESH
        )
    pl.semaphore_wait(barrier, len(devices))


def neighbours():
    _, me = place()
    return [{"front": lax.rem(me + 1, RING)}, {"front": lax.rem(me + 3, RING)}]


class Ring:
    def __init__(self, view, size, sems, sibling, own, lower):
        _, me = place()
        self.own, self.lower = own, lower
        self.view, self.size, self.sems, self.sibling = view, size, sems, sibling
        self.me = me
        self.right, self.left = lax.rem(me + 1, RING), lax.rem(me + 3, RING)
        self.across = lax.rem(me + 2, RING)

    def copy(self, k, c):
        part = self.size // 2
        to_right, to_left = {"front": self.right}, {"front": self.left}
        source, offset, rows, device = (
            (self.me, 0, part, to_right),
            (self.me, part, part, to_left),
            (self.me, part, part, to_right),
            (self.me, 0, part, to_left),
            (self.left, 0, part, to_right),
            (self.right, part, part, to_left),
            (self.me, 0, self.size, self.sibling),
            (self.left, 0, self.size, self.sibling),
            (self.right, 0, self.size, self.sibling),
            (self.across, 0, self.size, self.sibling),
        )[k]
        ref = self.view(source, offset, rows, c)
        return pltpu.make_async_remote_copy(
            src_ref=ref,
            dst_ref=ref,
            send_sem=self.sems.at[0, c, k],
            recv_sem=self.sems.at[1, c, k],
            device_id=device,
            device_id_type=pl.DeviceIdType.MESH,
        )

    def sent(self, k):
        return (
            self.me, self.me, self.me, self.me, self.left, self.right,
            self.me, self.left, self.right, self.across,
        )[k]

    def received(self, k):
        return (
            self.left, self.right, self.left, self.right, self.across, self.across,
            self.me, self.left, self.right, self.across,
        )[k]

    def act(self, source, c, action):
        if self.lower:
            pl.when(source >= c)(action)
        else:
            action()

    def start(self, k, c):
        self.act(self.sent(k), c, lambda: self.copy(k, c).start())

    def wait_recv(self, k, c):
        self.act(self.received(k), c, lambda: self.copy(k, c).wait_recv())

    def wait_send(self, k, c):
        self.act(self.sent(k), c, lambda: self.copy(k, c).wait_send())

    def begin(self, c):
        for k in range(4):
            self.start(k, c)
        if self.own:
            self.start(6, c)

    def forward(self, c):
        for k in range(4):
            self.wait_recv(k, c)
            if k < 2:
                self.start(4 + k, c)
            elif self.sibling is not None:
                self.start(5 + k, c)

    def finish(self, c):
        self.wait_recv(4, c)
        self.wait_recv(5, c)
        if self.sibling is not None:
            self.start(9, c)

    def settle(self, c):
        for k in range(10 if self.sibling is not None else 6):
            if k == 6 and not self.own:
                continue
            if k >= 6:
                self.wait_recv(k, c)
            self.wait_send(k, c)


def front_kernel(level, mask_ref, near_ref, own_ref, peer_ref, *refs):
    if level == 1:
        factor_ref, panels_ref, *refs = refs
    else:
        given_ref, factor_ref, panel_ref, panels_ref, taken_ref, given_buf, given_sems, *refs = refs
    (keep_ref, a_ref, high_ref, low_ref, inv_ref, near_top, init_top, far_top, near_rest, init_rest, far_rest,
     local_sems, top_sems, rest_sems, pivot_sems, panel_sems) = refs
    leaf, me = place()
    core = lax.rem(leaf, 2)
    sibling = {"leaf": leaf + 1 - 2 * core}
    bit = lax.rem(leaf // level, 2)
    partner = {"leaf": leaf + level * (1 - 2 * bit)}
    half = TILE // 2
    low = pl.multiple_of(core * half, half)
    mine = pl.ds(low, half)
    theirs = mine if level == 2 else pl.ds(pl.multiple_of(half - low, half), half)
    quarter = lax.rem(leaf, 4)

    def tile(c):
        return pl.ds(pl.multiple_of(c * TILE, TILE), TILE)

    loads = [
        pltpu.make_async_copy(near_ref.at[0], near_top, local_sems.at[0]),
        pltpu.make_async_copy(own_ref.at[0, mine], init_top.at[bit], local_sems.at[1]),
        pltpu.make_async_copy(peer_ref.at[0, mine], init_top.at[1 - bit], local_sems.at[2]),
        pltpu.make_async_copy(near_ref.at[pl.ds(1, 3)], near_rest, local_sems.at[3]),
        pltpu.make_async_copy(own_ref.at[pl.ds(1, 3)], init_rest.at[bit], local_sems.at[4]),
        pltpu.make_async_copy(peer_ref.at[pl.ds(1, 3)], init_rest.at[1 - bit], local_sems.at[5]),
    ]
    loads.append(pltpu.make_async_copy(mask_ref, keep_ref, local_sems.at[7]))
    if level == 2:
        loads.append(pltpu.make_async_copy(given_ref, given_buf, local_sems.at[6]))
    for load in loads:
        load.start()
    meet(neighbours() + [sibling] + ([partner] if level == 2 else []))

    def top_copy(c):
        return pltpu.make_async_remote_copy(
            src_ref=near_top.at[theirs, tile(c)],
            dst_ref=far_top.at[:, tile(c)],
            send_sem=top_sems.at[0, c],
            recv_sem=top_sems.at[1, c],
            device_id=partner,
            device_id_type=pl.DeviceIdType.MESH,
        )

    def rest_copy(c, k):
        if level == 1:
            source, target = near_rest.at[:, :, tile(c)], far_rest.at[:, :, tile(c)]
        elif k == 0:
            source, target = near_rest.at[:, mine, tile(c)], far_rest.at[:, mine, tile(c)]
        else:
            source = target = far_rest.at[:, mine, tile(c)]
        return pltpu.make_async_remote_copy(
            src_ref=source,
            dst_ref=target,
            send_sem=rest_sems.at[0, c, k],
            recv_sem=rest_sems.at[1, c, k],
            device_id=partner if k == 0 else sibling,
            device_id_type=pl.DeviceIdType.MESH,
        )

    def rest_onward(c):
        if level == 2:
            rest_copy(c, 0).wait_recv()
            rest_copy(c, 1).start()

    pivots = Ring(
        lambda source, offset, rows, c: a_ref.at[
            pl.ds(pl.multiple_of(source * TILE + low + offset, half // 2), rows), tile(c)
        ],
        half,
        pivot_sems,
        sibling,
        True,
        True,
    )
    share = C // 2 if level == 1 else TILE
    base = core * share if level == 1 else 0
    panels = Ring(
        lambda source, offset, rows, c: panels_ref.at[
            source, pl.ds(pl.multiple_of(base + offset, share // 2), rows), tile(c)
        ],
        share,
        panel_sems,
        sibling if level == 1 else None,
        False,
        False,
    )

    def give():
        return pltpu.make_async_remote_copy(
            src_ref=given_buf,
            dst_ref=taken_ref,
            send_sem=given_sems.at[0],
            recv_sem=given_sems.at[1],
            device_id=partner,
            device_id_type=pl.DeviceIdType.MESH,
        )

    loads[0].wait()
    for c in range(ST):
        top_copy(c).start()
    loads[1].wait()
    loads[2].wait()
    own_rows = pl.ds(pl.multiple_of(me * TILE + low, half), half)
    for c in range(ST):
        top_copy(c).wait_recv()
        there = slice(c * TILE, (c + 1) * TILE)
        a_ref[own_rows, there] = (
            near_top[mine, there].astype(F32)
            + far_top[:, there].astype(F32)
            + init_top[c // 2, :, (c % 2) * TILE : (c % 2 + 1) * TILE].astype(F32)
        )
        if c == 0:
            pivots.begin(0)
    for load in loads[3:]:
        load.wait()
    for c in range(ST):
        rest_copy(c, 0).start()
    pivots.forward(0)
    pivots.begin(1)
    rest_onward(0)
    pivots.finish(0)

    def arrive(c):
        pivots.settle(c)
        rest_copy(c, 0).wait_send()
        if level == 2:
            rest_copy(c, 1).wait()
        else:
            rest_copy(c, 0).wait_recv()
        for m in range(3):
            rows = slice(S + m * TILE, S + (m + 1) * TILE)
            keep = keep_ref[4 * m + me, c, leaf // (2 * level)].astype(F32)
            a_ref[rows, tile(c)] = (
                near_rest[m, :, tile(c)].astype(F32)
                + far_rest[m, :, tile(c)].astype(F32)
                + init_rest[c // 2, m, :, tile(c % 2)].astype(F32) * keep
            )

    def left(rows, cols):
        return jnp.concatenate(
            [high_ref[rows, cols], low_ref[rows, cols], high_ref[rows, cols]], axis=1
        )

    def right(rows, cols):
        return jnp.concatenate(
            [high_ref[rows, cols], high_ref[rows, cols], low_ref[rows, cols]], axis=1
        )

    def step(g, _):
        c = g // 2
        even = g % 2 == 0
        odd = g % 2 == 1

        @pl.when(even)
        def _():
            arrive(c)

        for k in range(1, ST):

            @pl.when(g == 2 * k)
            def _():
                rows, done = slice(k * TILE, None), slice(0, k * TILE)
                there = slice(k * TILE, (k + 1) * TILE)
                a_ref[rows, there] -= (
                    dot_nt(high_ref[rows, done], high_ref[there, done])
                    + dot_nt(low_ref[rows, done], high_ref[there, done])
                    + dot_nt(high_ref[rows, done], low_ref[there, done])
                )

        cols = pl.ds(pl.multiple_of(g * G, G), G)
        invert_diagonal(a_ref.at[cols, cols], inv_ref)

        @pl.when(jnp.logical_and(even, g < 6))
        def _():
            pivots.forward(c + 1)
            rest_onward(c + 1)

        @pl.when(jnp.logical_and(even, g < 4))
        def _():
            pivots.begin(c + 2)

        if level == 2:

            @pl.when(g == 4)
            def _():
                give().start()

        @pl.when(jnp.logical_and(odd, g < 6))
        def _():
            pivots.finish(c + 1)

        inverse = right_parts(inv_ref[...])

        def panel(first, last):
            x = dot_nt(left_parts(a_ref[first:last, cols]), inverse)
            a_ref[first:last, cols] = x
            high, rest = split(x)
            high_ref[first:last, cols] = high
            low_ref[first:last, cols] = rest

        @pl.when(g < 4)
        def _():
            panel(0, S // 2)

        panel(S // 2, S + C)

        @pl.when(even)
        def _():
            after = pl.ds(pl.multiple_of(g * G + G, G), G)
            y = right(after, cols)

            def inside(first, last):
                a_ref[first:last, after] -= dot_nt(left(slice(first, last), cols), y)

            @pl.when(g < 4)
            def _():
                inside(0, S // 2)

            inside(S // 2, S + C)

        @pl.when(jnp.logical_and(even, g > 1))
        def _():
            panels.forward(c - 1)

        @pl.when(odd)
        def _():
            if level == 1:
                panels_ref[me, :, tile(c)] = high_ref[S:, tile(c)]
            else:
                panel_ref[:, tile(c)] = high_ref[S:, tile(c)]
                column = lax.rem(me + quarter, RING)
                part = lax.min((3 * quarter + column) // 4, 2)
                rows = pl.ds(pl.multiple_of(S + part * TILE, TILE), TILE)
                panels_ref[me, :, tile(c)] = high_ref[rows, tile(c)]
            panels.begin(c)

        @pl.when(jnp.logical_and(odd, g > 1))
        def _():
            panels.finish(c - 1)

        return 0

    lax.fori_loop(0, S // G, step, 0)
    width = S // (2 * level)
    start = lax.rem(leaf, 2 * level) * width
    part = pl.ds(pl.multiple_of(start, width), width)
    row = lax.broadcasted_iota(jnp.int32, (TILE, width), 0) + me * TILE
    col = lax.broadcasted_iota(jnp.int32, (TILE, width), 1) + start
    factor_ref[0] = jnp.where(row >= col, a_ref[tile(me), part], 0.0)
    for m in range(1, 4):
        factor_ref[m] = a_ref[S + (m - 1) * TILE : S + m * TILE, part]
    panels.forward(ST - 1)
    panels.finish(ST - 1)
    for c in range(ST):
        panels.settle(c)
        top_copy(c).wait_send()
    if level == 2:
        give().wait()


def front(level, tile_mask, near, own, peer, given=None):
    hbm = pl.BlockSpec(memory_space=pl.ANY)
    vmem = pl.BlockSpec(memory_space=pltpu.VMEM)
    width = S // (2 * level)
    half = TILE // 2
    factor = jax.ShapeDtypeStruct((4, TILE, width), F32)
    if level == 1:
        outs = [factor, jax.ShapeDtypeStruct((RING, C, S), BF16)]
    else:
        outs = [
            factor,
            jax.ShapeDtypeStruct((C, S), BF16),
            jax.ShapeDtypeStruct((RING, TILE, S), BF16),
            jax.ShapeDtypeStruct((3, TILE, C), BF16),
        ]
    given = [] if level == 1 else [given]
    return pl.pallas_call(
        functools.partial(front_kernel, level),
        out_shape=outs,
        in_specs=[hbm] * (4 + len(given)),
        out_specs=[vmem] * len(outs),
        scratch_shapes=[
            *([pltpu.VMEM((3, TILE, C), BF16), pltpu.SemaphoreType.DMA((2,))] if given else []),
            pltpu.SMEM(tile_mask.shape, jnp.int32),
            pltpu.VMEM((S + C, S), F32),
            pltpu.VMEM((S + C, S), BF16),
            pltpu.VMEM((S + C, S), BF16),
            pltpu.VMEM((G, G), F32),
            pltpu.VMEM((TILE, S), BF16),
            pltpu.VMEM((2, half, S // 2), BF16),
            pltpu.VMEM((half, S), BF16),
            pltpu.VMEM((3, TILE, S), BF16),
            pltpu.VMEM((2, 3, TILE, S // 2), BF16),
            pltpu.VMEM((3, TILE, S), BF16),
            pltpu.SemaphoreType.DMA((8,)),
            pltpu.SemaphoreType.DMA((2, ST)),
            pltpu.SemaphoreType.DMA((2, ST, 2)),
            pltpu.SemaphoreType.DMA((2, ST, 10)),
            pltpu.SemaphoreType.DMA((2, ST, 10)),
        ],
        compiler_params=pltpu.CompilerParams(
            collective_id=level, has_side_effects=True, vmem_limit_bytes=VMEM_LIMIT
        ),
        cost_estimate=pl.CostEstimate(
            flops=50_000_000_000, bytes_accessed=20_000_000, transcendentals=0
        ),
        name=f"front_{level}",
    )(tile_mask, near, own, peer, *given)


def update_one_kernel(ones_ref, twos_ref, panels_ref, own_ref, peer_ref, pivot_out, near_out, far_out,
                      one_ref, two_ref, x_buf, y_buf, tiles, total_ref, sems, x_sem, map_sems):
    leaf, group = place()
    quarter = leaf % 4
    across = (quarter + 2) % 4
    sides = (own_ref, peer_ref)
    x_copy = pltpu.make_async_copy(panels_ref.at[group], x_buf, x_sem)
    x_copy.start()
    pair = leaf // 2
    fetches = [
        pltpu.make_async_copy(ones_ref, one_ref, map_sems.at[0]),
        pltpu.make_async_copy(twos_ref, two_ref, map_sems.at[1]),
    ]
    for fetch in fetches:
        fetch.start()
    for fetch in fetches:
        fetch.wait()

    def column(i):
        t = jnp.where(i < 4, i, jnp.where(i < 7, 3 * quarter + i, 3 * across + i - 3))
        tile, live = source_of(two_ref, pair, t % 4, t // 4)
        return t % 4, tile, live

    def there(i):
        return pl.ds(pl.multiple_of(i * TILE, TILE), TILE)

    def copy(source, target, i, k):
        return pltpu.make_async_copy(source, target, sems.at[i, k])

    rows = [[source_of(one_ref, leaf ^ side, group, 1 + s) for s in range(3)] for side in (0, 1)]
    targets = [source_of(two_ref, pair, group, m) for m in range(4)]

    def start(i, _):
        other, tile, _ = column(i)
        copy(panels_ref.at[other, there(tile)], y_buf.at[i], i, 0).start()
        for side in (0, 1):
            col, _ = source_of(one_ref, leaf ^ side, other, 1 + tile)
            for s in range(3):
                copy(
                    sides[side].at[rows[side][s][0], :, there(col * 4 + other)],
                    tiles.at[side, s, :, there(i)],
                    i,
                    1 + 3 * side + s,
                ).start()
        return 0

    lax.fori_loop(0, 10, start, 0)
    x_copy.wait()

    def step(i, _):
        other, tile, col_live = column(i)
        copy(panels_ref.at[0, there(0)], y_buf.at[i], i, 0).wait()
        product = dot_nt(x_buf[...], y_buf[i])
        for s in range(3):
            total = -product[s * TILE : (s + 1) * TILE, :]
            for side in (0, 1):
                slot = tiles.at[side, s, :, there(i)]
                copy(own_ref.at[0, :, there(0)], slot, i, 1 + 3 * side + s).wait()
                _, live = source_of(one_ref, leaf ^ side, other, 1 + tile)
                live = jnp.logical_and(rows[side][s][1], live)
                total = total + jnp.where(live, slot[...].astype(F32), 0.0)
            total_ref[s] = total.astype(BF16)

        def target(m, out, to, at):
            live = jnp.logical_and(targets[m][1], col_live)

            @pl.when(live)
            def _():
                out[to, :, there(at)] = total_ref[targets[m][0]]

            @pl.when(jnp.logical_not(live))
            def _():
                out[to, :, there(at)] = jnp.zeros((TILE, TILE), BF16)

        @pl.when(i < 4)
        def _():
            for m in range(4):
                target(m, pivot_out, m, i)

        @pl.when(jnp.logical_and(i >= 4, i < 7))
        def _():
            for m in range(1, 4):
                target(m, near_out, m - 1, i - 4)

        @pl.when(i >= 7)
        def _():
            for m in range(1, 4):
                target(m, far_out, m - 1, i - 7)

        return 0

    lax.fori_loop(0, 10, step, 0)


def update_one_rows(map_one, map_two, panels, own, peer):
    hbm = pl.BlockSpec(memory_space=pl.ANY)
    return pl.pallas_call(
        update_one_kernel,
        out_shape=[
            jax.ShapeDtypeStruct((4, TILE, S), BF16),
            jax.ShapeDtypeStruct((3, TILE, C), BF16),
            jax.ShapeDtypeStruct((3, TILE, C), BF16),
        ],
        in_specs=[hbm] * 5,
        scratch_shapes=[
            pltpu.SMEM(map_one.shape, jnp.int32),
            pltpu.SMEM(map_two.shape, jnp.int32),
            pltpu.VMEM((C, S), BF16),
            pltpu.VMEM((10, TILE, S), BF16),
            pltpu.VMEM((2, 3, TILE, 10 * TILE), BF16),
            pltpu.VMEM((3, TILE, TILE), BF16),
            pltpu.SemaphoreType.DMA((10, 7)),
            pltpu.SemaphoreType.DMA,
            pltpu.SemaphoreType.DMA((2,)),
        ],
        compiler_params=pltpu.CompilerParams(vmem_limit_bytes=VMEM_LIMIT),
        name="update_1",
    )(map_one, map_two, panels, own, peer)


def update_two_kernel(x_ref, y_ref, near_ref, far_ref, one_in, two_in, out_ref, one_out, two_out,
                      one_buf, two_buf, sems):
    copies = [
        pltpu.make_async_copy(one_in, one_buf, sems.at[0]),
        pltpu.make_async_copy(two_in, two_buf, sems.at[1]),
        pltpu.make_async_copy(one_buf, one_out, sems.at[2]),
        pltpu.make_async_copy(two_buf, two_out, sems.at[3]),
    ]
    for copy in copies[:2]:
        copy.start()
    leaf, _ = place()
    quarter = lax.rem(leaf, 4)
    for i in range(3):
        there = slice(i * TILE, (i + 1) * TILE)
        product = dot_nt(x_ref[...], y_ref[lax.rem(3 * quarter + i, RING)])
        for m in range(3):
            front = near_ref[m, :, there].astype(F32) + far_ref[m, :, there].astype(F32)
            out_ref[m, :, there] = (front - product[m * TILE : (m + 1) * TILE, :]).astype(BF16)
        if i == 0:
            for k in (0, 1):
                copies[k].wait()
                copies[k + 2].start()
    for copy in copies[2:]:
        copy.wait()


def update_two_rows(panel, panels, near, far, factor_one, factor_two):
    vmem = pl.BlockSpec(memory_space=pltpu.VMEM)
    hbm = pl.BlockSpec(memory_space=pl.ANY)
    return pl.pallas_call(
        update_two_kernel,
        out_shape=[
            jax.ShapeDtypeStruct((3, TILE, C), BF16),
            jax.ShapeDtypeStruct(factor_one.shape, F32),
            jax.ShapeDtypeStruct(factor_two.shape, F32),
        ],
        in_specs=[vmem] * 4 + [hbm] * 2,
        out_specs=[vmem, hbm, hbm],
        scratch_shapes=[
            pltpu.VMEM(factor_one.shape, F32),
            pltpu.VMEM(factor_two.shape, F32),
            pltpu.SemaphoreType.DMA((4,)),
        ],
        compiler_params=pltpu.CompilerParams(vmem_limit_bytes=VMEM_LIMIT),
        name="update_2",
    )(panel, panels, near, far, factor_one, factor_two)


def join_halves(mine, other, position):
    lower_first = jnp.concatenate([mine, other], axis=-1)
    upper_first = jnp.concatenate([other, mine], axis=-1)
    return jnp.where(position == 0, lower_first, upper_first)


def body(child_update, sep_one, sep_two, map_one, map_two, mask_one, mask_two):
    leaf = lax.axis_index("leaf")
    own = child_update[0, 0, 0]
    entries = sep_one[0, 0, 0]
    quarter = sep_two[0, 0, 0]
    map_one, map_two = map_one[:, 0].transpose(2, 1, 0), map_two[:, 0].transpose(2, 1, 0)
    mask_one, mask_two = mask_one[:, 0].transpose(1, 2, 0), mask_two[:, 0].transpose(1, 2, 0)
    entries_peer, quarter_peer, peer = swapped((entries, quarter, own), "leaf", 0)
    near = spread(map_one, own)
    half = join_halves(quarter, quarter_peer, leaf % 2)
    half_far = swapped(half, "leaf", 1)
    factor_one, panels = front(1, mask_one, near, entries, entries_peer)
    panels, half, half_far = lax.optimization_barrier((panels, half, half_far))
    near, rest, given = update_one_rows(map_one, map_two, panels, own, peer)
    factor_two, panel, panels, taken = front(2, mask_two, near, half, half_far, given)
    update_two, factor_one, factor_two = update_two_rows(
        panel, panels, rest, taken, factor_one, factor_two
    )
    return (factor_one[None, None, None], factor_two[None, None, None], update_two[None, None, None])


def solution(mesh):
    split_spec = P("leaf", "front", None, None, None, None)
    return jax.shard_map(
        body,
        mesh=mesh,
        in_specs=(split_spec, split_spec, split_spec, P(), P(), P(), P()),
        out_specs=(split_spec, split_spec, split_spec),
        check_vma=False,
    )
```
